32 devices in a mesh: cables: 2 (over x), chan: 16 (over z, y, core).
Axes of the slice: x: 2, y: 2, z: 4, core: 2. Of those that a mesh axis runs over, the one named last changes fastest.
Arguments:
- traces: bfloat16 [4096, 128], P(('cables', 'chan')), parts along dimension 0, may hold values from -30 to 30
- filter_coefs: float32 [16, 5], replicated, may hold values from -2 to 2, as said below
- leakage: bfloat16 [4096, 16], P(('cables', 'chan')), parts along dimension 0, may hold values from 0 to 1
- live_mask: int32 [4096], P(('cables', 'chan')), parts along dimension 0, may hold values 0 or 1
- aperture_starts: int32 [32], P(('cables', 'chan')), parts along dimension 0, may hold values from 0 to 2047, as said below
- delays: int32 [256, 512], replicated, may hold values from 0 to 15
- refine_lists: int32 [32, 2, 8], P(('cables', 'chan')), parts along dimension 0, may hold values from 0 to 255
Outputs:
- beam_power: bfloat16 [32, 256, 16, 128], P(('cables', 'chan')), parts along dimension 0
- refined_power: bfloat16 [32, 2, 8, 16, 128], P(('cables', 'chan')), parts along dimension 0
The draws below stay inside these ranges and needn't reach their ends.
There are 2 independent parts, one for each index of `cables`. The reference program is written for one: setup_inputs(seed, part) draws one part's arguments, and reference() takes and returns one part's arrays. A program takes and returns all parts, laid end to end along the dimension named above; an argument that names none is the same for every part. Nothing has to cross between parts.
Inputs may be any that keep to these rules, and one draw needn't show every extreme that they name: `aperture_starts`: aperture a begins at one of the 128 channels of block a // 1 of the cable (channels (a) * 128 up to that plus 128 - 1). `filter_coefs`: each band is a stable bandpass biquad.
All inputs are finite; a program needn't handle non-finite values. No bound on the sum of `live_mask` on one device may be relied on, other than what follows from the above.
Results may differ from the reference program's by a relative error of at most 0.0065.
Values may be sent and summed in bfloat16 or wider, within the bound.
A program may use at most 192 MiB of HBM per device.

```python
import math
import jax
import jax.numpy as jnp
from jax import lax

CH_DEV = 128
NT = 128
NB = 16
NP = 256
AP = 512
DMAX = 16
R = 8
PASSES = 2
A_DEV = 1
FIBRE_TAPS = 2048
NA = 16


def draw_traces(key, part):
    key_gain, key_common, key_noise = jax.random.split(key, 3)
    low_end = math.log(0.3)
    gains = jnp.exp(jax.random.uniform(key_gain, (FIBRE_TAPS, 1), jnp.float32, low_end, math.log(3.0)))
    common = jax.random.normal(key_common, (1, NT), jnp.float32)
    jitter_noise = jax.random.normal(key_noise, (FIBRE_TAPS, NT), jnp.float32)
    return jnp.clip(gains * (common + jitter_noise), -30.0, 30.0).astype(jnp.bfloat16)


def draw_filter_coefs(key, part):
    key_freq, key_width = jax.random.split(key)
    centre = jnp.exp(jax.random.uniform(key_freq, (NB,), jnp.float32, math.log(0.01), math.log(0.25)))
    quality = jax.random.uniform(key_width, (NB,), jnp.float32, 0.7, 4.0)
    angular = 2.0 * math.pi * centre
    spread = jnp.sin(angular) / (2.0 * quality)
    leading = 1.0 + spread
    return jnp.stack([spread / leading, jnp.zeros_like(leading), -spread / leading, -2.0 * jnp.cos(angular) / leading, (1.0 - spread) / leading], axis=1).astype(jnp.float32)


def draw_leakage(key, part):
    random_seed_list = jax.random.split(key, 8)
    order = jax.random.permutation(random_seed_list[0], NB)
    fast_count = jax.random.randint(random_seed_list[1], (), NB // 4, NB // 2 + 1)
    is_fast = order < fast_count
    quick_rate = jnp.exp(jax.random.uniform(random_seed_list[2], (NB,), jnp.float32, math.log(1.0 / 50.0), math.log(1.0 / 30.0)))
    slow_rate = jax.random.uniform(random_seed_list[3], (NB,), jnp.float32, 0.2, 0.6) / FIBRE_TAPS
    background_speed = jnp.where(is_fast, quick_rate, slow_rate)
    device_factor = jnp.exp(jax.random.uniform(random_seed_list[4], (FIBRE_TAPS // CH_DEV,), jnp.float32, math.log(0.7), math.log(1.4)))
    tap_readings = device_factor[jnp.arange(FIBRE_TAPS) // CH_DEV][:, None]
    rough_guess = jnp.exp(jax.random.uniform(random_seed_list[5], (FIBRE_TAPS, NB), jnp.float32, math.log(0.8), math.log(1.25)))
    transient_start = jax.random.randint(random_seed_list[6], (2,), 0, FIBRE_TAPS)
    transient_duration = jax.random.uniform(random_seed_list[7], (2,), jnp.float32, math.log(1.0 / 0.8), math.log(1.0 / 0.6))
    transient_onsets = jnp.sum((jnp.arange(FIBRE_TAPS)[:, None] == transient_start[None]).astype(jnp.float32) * transient_duration[None], axis=1)
    return (background_speed[None] * tap_readings * rough_guess + transient_onsets[:, None]).astype(jnp.bfloat16)


def draw_aperture_starts(key, part):
    owners = jnp.arange(NA) // A_DEV
    return (owners * CH_DEV + jax.random.randint(key, (NA,), 0, CH_DEV)).astype(jnp.int32)


def set_ends(array, stream_key, smallest, largest):
    longest = array.shape.index(max(array.shape))
    spots = []
    for shift in (0, 1):
        where = [jax.random.randint(jax.random.fold_in(stream_key, axis), (), 0, length) for axis, length in enumerate(array.shape)]
        where[longest] = (where[longest] + shift) % array.shape[longest]
        spots.append(tuple(where))
    return array.at[spots[0]].set(smallest).at[spots[1]].set(largest)


def setup_inputs(seed: int = 0, part: int = 0) -> dict:
    keys = jax.random.split(jax.random.key(seed), 8)
    part_keys = jax.random.split(jax.random.fold_in(keys[7], part), 8)
    traces = draw_traces(jax.random.fold_in(jax.random.fold_in(keys[7], part), 71), part)
    filter_coefs = draw_filter_coefs(jax.random.fold_in(keys[7], 71), part)
    leakage = draw_leakage(jax.random.fold_in(jax.random.fold_in(keys[7], part), 71), part)
    live_mask = set_ends((jax.random.randint(part_keys[3], (FIBRE_TAPS,), 0, 8) < 7).astype(jnp.int32), jax.random.fold_in(part_keys[3], 1), 0, 1)
    aperture_starts = draw_aperture_starts(jax.random.fold_in(jax.random.fold_in(keys[7], part), 71), part)
    delays = set_ends(jax.random.randint(keys[5], (NP, AP), 0, DMAX), jax.random.fold_in(keys[5], 1), 0, DMAX - 1).astype(jnp.int32)
    refine_lists = set_ends(jax.random.randint(part_keys[6], (NA, PASSES, R), 0, NP), jax.random.fold_in(part_keys[6], 1), 0, NP - 1).astype(jnp.int32)
    return dict(traces=traces, filter_coefs=filter_coefs, leakage=leakage, live_mask=live_mask, aperture_starts=aperture_starts, delays=delays, refine_lists=refine_lists)


eps_norm = 1e-06

def hilbert_table(samples):
    indices = jnp.arange(samples)
    offset = (indices[None, :] - indices[:, None]) % samples
    is_odd = offset % 2 == 1
    phases = jnp.pi * offset.astype(jnp.float32) / samples
    divisor = jnp.where(is_odd, jnp.sin(phases), 1.0)
    return jnp.where(is_odd, 2.0 / samples * jnp.cos(phases) / divisor, 0.0).astype(jnp.float32)

def envelope_power(signal, hilbert):
    turned = jnp.dot(signal, hilbert, precision=lax.Precision.HIGHEST, preferred_element_type=jnp.float32)
    return (signal * signal + turned * turned).astype(jnp.bfloat16)

def reference(traces, filter_coefs, leakage, live_mask, aperture_starts, delays, refine_lists):
    chan_count, samples = traces.shape
    band_count = filter_coefs.shape[0]
    b_zero = filter_coefs[:, 0]
    b_one = filter_coefs[:, 1]
    b_two = filter_coefs[:, 2]
    a_one = filter_coefs[:, 3]
    a_two = filter_coefs[:, 4]
    signal = traces.astype(jnp.float32)

    def advance(carry_state, in_now):
        in_last, in_before, out_last, out_before = carry_state
        out_now = b_zero * in_now[:, None] + b_one * in_last[:, None] + b_two * in_before[:, None] - a_one * out_last - a_two * out_before
        return ((in_now, in_last, out_now, out_last), out_now)
    flat_zero = jnp.zeros((chan_count,), jnp.float32)
    band_zero = jnp.zeros((chan_count, band_count), jnp.float32)
    _, response = lax.scan(advance, (flat_zero, flat_zero, band_zero, band_zero), signal.T)
    live_flag = live_mask.astype(jnp.float32)
    filtered = (live_flag[:, None, None] * jnp.transpose(response, (1, 2, 0))).astype(jnp.bfloat16)
    filtered = lax.optimization_barrier(filtered).astype(jnp.float32)
    leak_rate = leakage.astype(jnp.float32)
    retention = jnp.exp(-leak_rate)
    inflow = -jnp.expm1(-leak_rate)

    def follow(running_mean, inputs):
        filtered_now, keep_now, inflow_now = inputs
        running_mean = keep_now[:, None] * running_mean + inflow_now[:, None] * filtered_now
        return (running_mean, running_mean)
    _, running_mean = lax.scan(follow, jnp.zeros((band_count, samples), jnp.float32), (filtered, retention, inflow))
    detrended = (live_flag[:, None, None] * (filtered - running_mean)).astype(jnp.bfloat16)
    aperture_len = delays.shape[1]
    slowness_count = delays.shape[0]
    detrended = jnp.concatenate([detrended, jnp.zeros((aperture_len, band_count, samples), jnp.bfloat16)], axis=0)
    live_wide = jnp.concatenate([live_flag, jnp.zeros((aperture_len,), jnp.float32)])
    hilbert = hilbert_table(samples)
    time_index = jnp.arange(samples)
    slot_count = refine_lists.shape[2]

    def one_aperture(aperture):
        first_chan = aperture_starts[aperture].astype(jnp.int32)
        window = lax.dynamic_slice_in_dim(detrended, first_chan, aperture_len, 0).astype(jnp.float32)
        live_window = lax.dynamic_slice_in_dim(live_wide, first_chan, aperture_len, 0)
        padded = jnp.concatenate([jnp.zeros_like(window), window], axis=2)

        def add_channel(summed, inputs):
            channel_row, shift_now = inputs
            lookup = samples - shift_now[:, None] + time_index[None]
            return (summed + channel_row[:, lookup], None)
        summed, _ = lax.scan(add_channel, jnp.zeros((band_count, slowness_count, samples), jnp.float32), (padded, delays.T))
        stacked = jnp.transpose(summed, (1, 0, 2)) / math.sqrt(aperture_len)
        beam_out = envelope_power(stacked.reshape(-1, samples), hilbert).reshape(stacked.shape)
        guide_trace = stacked[refine_lists[aperture, 0]]
        pass_powers = []
        for pass_index in range(refine_lists.shape[1]):
            chosen = delays[refine_lists[aperture, pass_index]]
            lookup = samples - chosen[:, :, None] + time_index[None, None]
            full_shape = (slot_count, aperture_len, band_count, samples)
            aligned = jnp.take_along_axis(jnp.broadcast_to(padded[None], (slot_count,) + padded.shape), jnp.broadcast_to(lookup[:, :, None, :], full_shape), axis=3)
            guide_b = lax.optimization_barrier(guide_trace.astype(jnp.bfloat16)).astype(jnp.float32)
            numerator = jnp.einsum('rkbt,rbt->rk', aligned, guide_b)
            energy = lax.optimization_barrier(jnp.sum(aligned * aligned, axis=(2, 3)))
            guide_norm = jnp.sqrt(lax.optimization_barrier(jnp.sum(guide_b * guide_b, axis=(1, 2))) + eps_norm)
            coherence = numerator / (jnp.sqrt(energy + eps_norm) * guide_norm[:, None])
            weight = (live_window[None] * (0.25 + jnp.maximum(coherence, 0.0))).astype(jnp.bfloat16)
            weight = lax.optimization_barrier(weight).astype(jnp.float32)
            refined = jnp.einsum('rk,rkbt->rbt', weight, aligned)
            refined = refined / jnp.sqrt(1.0 + lax.optimization_barrier(jnp.sum(weight * weight, axis=1)))[:, None, None]
            pass_powers.append(envelope_power(refined.reshape(-1, samples), hilbert).reshape(refined.shape))
            guide_trace = refined
        return (beam_out, jnp.stack(pass_powers))
    return lax.map(one_aperture, jnp.arange(aperture_starts.shape[0]))
```

```python
import functools
import math

import numpy as np

import jax
import jax.numpy as jnp
from jax import lax
from jax.experimental import pallas as pl
from jax.experimental.pallas import tpu as pltpu
from jax.sharding import PartitionSpec as P

DMAX = 16
LANES = 128
EPS = 1e-06
MIB = 1024 * 1024
MESH = pl.DeviceIdType.MESH
VM = pl.BlockSpec(memory_space=pltpu.VMEM)
SM = pl.BlockSpec(memory_space=pltpu.SMEM)
HB = pl.BlockSpec(memory_space=pl.ANY)
F32 = jnp.float32
BF16 = jnp.bfloat16
NT_DIMS = (((1,), (1,)), ((), ()))


def hilbert_table(samples):
    index = np.arange(samples)
    offset = (index[:, None] - index[None, :]) % samples
    odd = offset % 2 == 1
    phase = np.pi * offset / samples
    table = np.where(odd, 2.0 / samples * np.cos(phase) / np.where(odd, np.sin(phase), 1.0), 0.0)
    return jnp.asarray(table.astype(np.float32).astype(jnp.bfloat16))


def inflow_of(leak):
    series = leak * (1.0 - leak * (0.5 - leak * (1.0 / 6.0 - leak * (1.0 / 24.0 - leak * (
        1.0 / 120.0 - leak * (1.0 / 720.0 - leak * (1.0 / 5040.0)))))))
    return jnp.where(leak < 0.5, series, 1.0 - jnp.exp(-leak))


def split(x):
    high = x.astype(BF16)
    low = (x - high.astype(F32)).astype(BF16)
    return high, low


def exchange_kernel(
    count, near, start_ref, x_ref, leak_ref, live_ref, coef_ref, delays_ref,
    packs_ref, inc_ref, toep_ref, hot_ref,
    pack, packs, msg, msgs, delt, s1, r1, s2, r2,
):
    chans, samples = x_ref.shape
    bands = leak_ref.shape[0]
    slow, aperture = delays_ref.shape
    me = lax.axis_index("chan")
    barrier = pltpu.get_barrier_semaphore()
    for i in range(1, count):
        pl.semaphore_signal(
            barrier, inc=1, device_id={"chan": lax.rem(me + i, count)}, device_id_type=MESH
        )

    lane = lax.broadcasted_iota(jnp.int32, (bands, chans), 1)
    live = jnp.broadcast_to(live_ref[...], (bands, chans)).astype(F32)
    pack[0:samples, :] = x_ref[...].astype(F32).T.astype(BF16)
    pack[samples : samples + bands, :] = leak_ref[...]
    pack[samples + bands : samples + 2 * bands, :] = live.astype(BF16)

    leak = leak_ref[...].astype(F32)
    inside = lane < start_ref[0] - me * chans
    leak_loc = jnp.where(inside, leak, 0.0)
    later = jnp.where(
        lax.broadcasted_iota(jnp.int32, (chans, chans), 0)
        > lax.broadcasted_iota(jnp.int32, (chans, chans), 1),
        1.0,
        0.0,
    ).astype(BF16)
    suffix = jnp.dot(
        jnp.concatenate([leak, leak_loc], axis=0).astype(BF16), later, preferred_element_type=F32
    )
    gain = inflow_of(leak) * live
    weights = jnp.concatenate([gain, jnp.where(inside, gain, 0.0)], axis=0) * jnp.exp(-suffix)
    high, low = split(weights)
    ends = jnp.dot(jnp.concatenate([high, low], axis=0), x_ref[...], preferred_element_type=F32)
    ends = ends[: 2 * bands] + ends[2 * bands :]
    total = jnp.broadcast_to(jnp.exp(-jnp.sum(leak, axis=1, keepdims=True)), (bands, chans))
    total_loc = jnp.exp(-jnp.sum(leak_loc, axis=1, keepdims=True))
    half = bands // 2
    msg[0:bands, :] = ends[:bands]
    msg[bands : bands + half, :] = jnp.where(lane[:half] < chans // 2, total[:half], total[half:])

    pl.semaphore_wait(barrier, count - 1)
    sends = []
    for i in range(1, count):
        sends.append(
            (
                pltpu.make_async_remote_copy(
                    src_ref=msg,
                    dst_ref=msgs.at[me],
                    send_sem=s1.at[i],
                    recv_sem=r1.at[i],
                    device_id={"chan": lax.rem(me + i, count)},
                    device_id_type=MESH,
                ),
                me + i < count,
                me - i >= 0,
            )
        )
        if i <= near:
            sends.append(
                (
                    pltpu.make_async_remote_copy(
                        src_ref=pack,
                        dst_ref=packs.at[i - 1],
                        send_sem=s2.at[i],
                        recv_sem=r2.at[i],
                        device_id={"chan": lax.rem(me + count - i, count)},
                        device_id_type=MESH,
                    ),
                    me - i >= 0,
                    me + i < count,
                )
            )
    for copy, sending, _ in sends:
        pl.when(sending)(copy.start)

    eye = lax.broadcasted_iota(jnp.int32, (bands, bands), 0) == lax.broadcasted_iota(
        jnp.int32, (bands, bands), 1
    )
    b0, b1, b2, a1, a2 = [
        jnp.sum(jnp.where(eye, coef_ref[i : i + 1, :], 0.0), axis=1, keepdims=True) for i in range(5)
    ]
    last = samples - 1
    time = last - lax.broadcasted_iota(jnp.int32, (bands, samples), 1)

    def delayed(v, n):
        return jnp.where(time >= n, pltpu.roll(v, samples - n, 1), 0.0)

    resp = jnp.where(time == 0, 1.0, 0.0)
    before = jnp.zeros((bands, 1), F32)
    size = 1
    while size < samples:
        newest = resp[:, samples - size : samples - size + 1]
        following = -a1 * newest - a2 * before
        grown = following * resp - a2 * newest * delayed(resp, 1)
        resp = jnp.where(time < size, resp, delayed(grown, size))
        before = resp[:, samples - 2 * size + 1 : samples - 2 * size + 2]
        size *= 2
    resp = b0 * resp + b1 * delayed(resp, 1) + b2 * delayed(resp, 2)

    def toep_row(t, _):
        row = jnp.where(last - time <= t, pltpu.roll(resp, t + 1, 1), 0.0)
        high, low = split(row)
        at = pl.ds(pl.multiple_of(t * bands, bands), bands)
        toep_ref[at, 0:samples] = high
        toep_ref[at, samples : 2 * samples] = low
        return 0

    lax.fori_loop(0, samples, toep_row, 0, unroll=8)

    delt[...] = delays_ref[...].T

    def hot_rows(d, _):
        at = pl.ds(pl.multiple_of(d * aperture, aperture), aperture)
        hot_ref[at, :] = jnp.where(delt[...] == d, 1.0, 0.0).astype(BF16)
        return 0

    lax.fori_loop(0, DMAX, hot_rows, 0)

    packs_ref[0] = pack[...]
    for copy, sending, receiving in sends:
        pl.when(sending)(copy.wait_send)
        pl.when(receiving)(copy.wait_recv)
    for i in range(1, near + 1):

        @pl.when(me + i < count)
        def _(i=i):
            packs_ref[i] = packs[i - 1]

        @pl.when(me + i >= count)
        def _(i=i):
            packs_ref[i] = jnp.zeros(packs_ref.shape[1:], BF16)

    def add_device(i, state):
        tile = msgs[i, bands : bands + half, :]
        keep = jnp.concatenate([tile[:, 0:1], tile[:, chans // 2 : chans // 2 + 1]], axis=0)
        return keep * state + msgs[i, 0:bands, :]

    incoming = lax.fori_loop(0, me, add_device, jnp.zeros((bands, samples), F32))
    inc_ref[...] = total_loc * incoming + ends[bands:]


def main_kernel(
    dims, start_ref, lists_ref, packs_ref, inc_ref, toep_ref, hot_ref, delays_ref, hilbert_ref,
    out_ref, out2_ref, xt, stacked, acc, acc2, power, power2,
):
    samples, bands, chans = dims
    slow, aperture = delays_ref.shape
    blocks = aperture // chans
    offset = lax.rem(start_ref[0], chans)
    points = samples * bands
    lead = (DMAX - 1) * bands
    passes, slots = lists_ref.shape

    rows = packs_ref.shape[1]
    lane = lax.broadcasted_iota(jnp.int32, (rows, chans), 1)
    turned = [pltpu.roll(packs_ref[j].astype(F32), chans - offset, 1) for j in range(blocks + 1)]
    window = [
        jnp.where(lane < chans - offset, turned[j], turned[j + 1]) for j in range(blocks)
    ]
    ones = lax.broadcasted_iota(jnp.int32, (chans, chans), 0) <= lax.broadcasted_iota(
        jnp.int32, (chans, chans), 1
    )
    tri = jnp.where(ones, 1.0, 0.0).astype(BF16)
    rise, fall, decay, live = [], [], [], []
    for j in range(blocks):
        leak = window[j][samples : samples + bands]
        live.append(window[j][samples + bands :])
        summed = jnp.dot(leak.astype(BF16), tri, preferred_element_type=F32)
        middle = 0.5 * summed[:, chans - 1 : chans]
        rise.append(jnp.exp(summed - middle) * inflow_of(leak))
        fall.append(jnp.exp(middle - summed))
        decay.append(jnp.exp(-summed))
    alive = jnp.concatenate(
        [window[j][:samples] * live[j][0:1, :] for j in range(blocks)], axis=1
    ).astype(BF16)
    stacked[0:samples, :] = alive
    stacked[samples : 2 * samples, :] = alive
    incoming = inc_ref[...]
    tri_wide = jnp.concatenate(
        [
            jnp.concatenate([tri, jnp.zeros_like(tri)], axis=1),
            jnp.concatenate([jnp.zeros_like(tri), tri], axis=1),
        ],
        axis=0,
    )
    xt[0:lead, :] = jnp.zeros((lead, aperture), BF16)
    tile = DMAX

    def filter_tile(i, energy, snaps=None):
        at = pl.multiple_of(i * (tile * bands), tile * bands)
        taps = toep_ref[pl.ds(at, tile * bands), :]
        filtered = jnp.dot(taps, stacked[...], preferred_element_type=F32)
        filtered = filtered.astype(BF16).astype(F32)
        rising = jnp.concatenate([jnp.concatenate(rise, axis=1)] * tile, axis=0)
        lifted = (filtered * rising).astype(BF16)
        wide = 2 * chans
        sums = [
            jnp.dot(lifted[:, n * wide : (n + 1) * wide], tri_wide, preferred_element_type=F32)
            for n in range(blocks // 2)
        ]
        taps = taps[:, :samples].astype(F32) + taps[:, samples:].astype(F32)
        energy = list(energy)
        for k in range(tile):
            part = slice(k * bands, (k + 1) * bands)
            carry = jnp.broadcast_to(
                jnp.sum(taps[part] * incoming, axis=1, keepdims=True), (bands, chans)
            )
            row = pl.ds(pl.multiple_of(lead + at + k * bands, bands), bands)
            for j in range(blocks):
                cols = slice(j * chans, (j + 1) * chans)
                inner = (j % 2) * chans
                mean = fall[j] * sums[j // 2][part, inner : inner + chans] + decay[j] * carry
                if j + 1 < blocks:
                    carry = jnp.broadcast_to(mean[:, chans - 1 : chans], (bands, chans))
                d = (live[j] * (filtered[part, cols] - mean)).astype(BF16)
                xt[row, cols] = d
                d = d.astype(F32)
                energy[j] = energy[j] + d * d
            if snaps is not None:
                snaps.append(
                    jnp.concatenate([jnp.sum(e, axis=0, keepdims=True) for e in energy], axis=1)
                )
        return tuple(energy)

    energy = tuple(jnp.zeros((bands, chans), F32) for _ in range(blocks))
    energy = lax.fori_loop(0, samples // tile - 1, filter_tile, energy)
    snaps = []
    filter_tile(samples // tile - 1, energy, snaps)
    norms = snaps[::-1]

    step = points // 2
    tiles = slow // LANES
    scale = 1.0 / math.sqrt(aperture)

    def stack(i, _):
        at = pl.multiple_of(i * step, step)
        lagged = jnp.concatenate(
            [
                xt[pl.ds(pl.multiple_of(at + (DMAX - 1 - d) * bands, bands), step), :]
                for d in range(DMAX)
            ],
            axis=1,
        )
        beams = jnp.dot(lagged, hot_ref[...], preferred_element_type=F32) * scale
        for j in range(tiles):
            acc[j, pl.ds(at, step), :] = beams[:, j * LANES : (j + 1) * LANES]
        return 0

    lax.fori_loop(0, points // step, stack, 0)

    pad = jnp.zeros((slots, DMAX * bands), F32)
    length = points + DMAX * bands
    slow_id = lax.broadcasted_iota(jnp.int32, (1, slow), 1)
    onehot = jnp.concatenate(
        [jnp.where(slow_id == lists_ref[0, r], 1.0, 0.0) for r in range(slots)], axis=0
    ).astype(BF16)
    beams = jnp.concatenate([acc[j].astype(BF16) for j in range(tiles)], axis=1)
    guide = lax.dot_general(onehot, beams, NT_DIMS, preferred_element_type=F32)
    mask = jnp.concatenate([v[0:1, :] for v in live], axis=1)
    results = []
    for i in range(passes):
        chosen = jnp.concatenate(
            [delays_ref[pl.ds(lists_ref[i, r], 1), :] for r in range(slots)], axis=0
        )
        guide = guide.astype(BF16).astype(F32)
        padded = jnp.concatenate([guide, pad], axis=1)
        shifted = [padded[:, :points]] + [
            pltpu.roll(padded, length - d * bands, 1)[:, :points] for d in range(1, DMAX)
        ]
        shifted = jnp.concatenate(shifted, axis=0).astype(BF16)
        products = jnp.dot(shifted, xt[lead : lead + points, :], preferred_element_type=F32)
        numerator = jnp.zeros((slots, aperture), F32)
        strength = jnp.zeros((slots, aperture), F32)
        for d in range(DMAX):
            match = chosen == d
            numerator = numerator + jnp.where(match, products[d * slots : (d + 1) * slots, :], 0.0)
            strength = strength + jnp.where(match, norms[d], 0.0)
        guide_norm = jnp.sqrt(jnp.sum(guide * guide, axis=1, keepdims=True) + EPS)
        coherence = numerator / (jnp.sqrt(strength + EPS) * guide_norm)
        weight = (mask * (0.25 + jnp.maximum(coherence, 0.0))).astype(BF16).astype(F32)
        spread = jnp.concatenate(
            [jnp.where(chosen == d, weight, 0.0) for d in range(DMAX)], axis=0
        ).astype(BF16)
        parts = lax.dot_general(
            spread, xt[lead : lead + points, :], NT_DIMS, preferred_element_type=F32
        )
        refined = parts[0:slots, :]
        for d in range(1, DMAX):
            part = jnp.concatenate([parts[d * slots : (d + 1) * slots, :], pad], axis=1)
            refined = refined + pltpu.roll(part, d * bands, 1)[:, :points]
        refined = refined / jnp.sqrt(1.0 + jnp.sum(weight * weight, axis=1, keepdims=True))
        results.append(refined)
        guide = refined
    total = passes * slots
    results.append(jnp.zeros((LANES - total, points), F32))
    acc2[...] = jnp.concatenate(results, axis=0).T

    def envelope(band, _):
        s = jnp.concatenate(
            [acc.at[j][pl.ds(band, samples, stride=bands), :] for j in range(tiles)]
            + [acc2[pl.ds(band, samples, stride=bands), :]],
            axis=1,
        )
        turned = jnp.dot(hilbert_ref[...], s.astype(BF16), preferred_element_type=F32)
        both = (s * s + turned * turned).T
        power[pl.ds(band, slow, stride=bands), :] = both[:slow]
        power2[pl.ds(band, total, stride=bands), :] = both[slow : slow + total]
        return 0

    lax.fori_loop(0, bands, envelope, 0)
    out_ref[...] = power[...].astype(BF16)
    out2_ref[...] = power2[...].astype(BF16)


def per_device(traces, filter_coefs, leakage, live_mask, aperture_starts, delays, refine_lists):
    chans, samples = traces.shape
    bands = filter_coefs.shape[0]
    slow, aperture = delays.shape
    near = (aperture + chans - 1) // chans
    count = lax.axis_size("chan")
    passes, slots = refine_lists.shape[1:]
    points = samples * bands
    rows = samples + 2 * bands
    dma = pltpu.SemaphoreType.DMA
    packs, inc, toep, hot = pl.pallas_call(
        functools.partial(exchange_kernel, count, near),
        out_shape=(
            jax.ShapeDtypeStruct((near + 1, rows, chans), BF16),
            jax.ShapeDtypeStruct((bands, samples), F32),
            jax.ShapeDtypeStruct((points, 2 * samples), BF16),
            jax.ShapeDtypeStruct((DMAX * aperture, slow), BF16),
        ),
        in_specs=[SM] + [VM] * 5,
        out_specs=(VM,) * 4,
        scratch_shapes=[
            pltpu.VMEM((rows, chans), BF16),
            pltpu.VMEM((near, rows, chans), BF16),
            pltpu.VMEM((bands + bands // 2, samples), F32),
            pltpu.VMEM((count, bands + bands // 2, samples), F32),
            pltpu.VMEM((aperture, slow), jnp.int32),
            dma((count,)), dma((count,)), dma((near + 1,)), dma((near + 1,)),
        ],
        compiler_params=pltpu.CompilerParams(
            collective_id=0, has_side_effects=True, vmem_limit_bytes=12 * MIB
        ),
    )(aperture_starts, traces, leakage.T, live_mask[None, :], filter_coefs.T, delays)
    beam, refined = pl.pallas_call(
        functools.partial(main_kernel, (samples, bands, chans)),
        out_shape=(
            jax.ShapeDtypeStruct((slow * bands, samples), BF16),
            jax.ShapeDtypeStruct((passes * slots * bands, samples), BF16),
        ),
        in_specs=[SM, SM] + [VM] * 6,
        out_specs=(VM, VM),
        scratch_shapes=[
            pltpu.VMEM((points + (DMAX - 1) * bands, aperture), BF16),
            pltpu.VMEM((2 * samples, aperture), BF16),
            pltpu.VMEM((slow // LANES, points, LANES), F32),
            pltpu.VMEM((points, LANES), F32),
            pltpu.VMEM((slow * bands, samples), F32),
            pltpu.VMEM((passes * slots * bands, samples), F32),
        ],
        compiler_params=pltpu.CompilerParams(vmem_limit_bytes=32 * MIB),
    )(aperture_starts, refine_lists[0], packs, inc, toep, hot, delays, hilbert_table(samples))
    return (
        beam.reshape(1, slow, bands, samples),
        refined.reshape(1, passes, slots, bands, samples),
    )


def solution(mesh):
    return jax.shard_map(
        per_device,
        mesh=mesh,
        in_specs=(
            P(("cables", "chan"), None),
            P(),
            P(("cables", "chan"), None),
            P(("cables", "chan")),
            P(("cables", "chan")),
            P(),
            P(("cables", "chan"), None, None),
        ),
        out_specs=(
            P(("cables", "chan"), None, None, None),
            P(("cables", "chan"), None, None, None, None),
        ),
        check_vma=False,
    )
```

```python
import functools
import math

import numpy as np

import jax
import jax.numpy as jnp
from jax import lax
from jax.experimental import pallas as pl
from jax.experimental.pallas import tpu as pltpu
from jax.sharding import PartitionSpec as P

DMAX = 16
LANES = 128
EPS = 1e-06
MIB = 1024 * 1024
MESH = pl.DeviceIdType.MESH
VM = pl.BlockSpec(memory_space=pltpu.VMEM)
SM = pl.BlockSpec(memory_space=pltpu.SMEM)
HB = pl.BlockSpec(memory_space=pltpu.HBM)
F32 = jnp.float32
BF16 = jnp.bfloat16
NT_DIMS = (((1,), (1,)), ((), ()))


def hilbert_table(samples):
    index = np.arange(samples)
    offset = (index[:, None] - index[None, :]) % samples
    odd = offset % 2 == 1
    phase = np.pi * offset / samples
    table = np.where(odd, 2.0 / samples * np.cos(phase) / np.where(odd, np.sin(phase), 1.0), 0.0)
    return jnp.asarray(table.astype(np.float32).astype(jnp.bfloat16))


def inflow_of(leak):
    series = leak * (1.0 - leak * (0.5 - leak * (1.0 / 6.0 - leak * (1.0 / 24.0 - leak * (
        1.0 / 120.0 - leak * (1.0 / 720.0 - leak * (1.0 / 5040.0)))))))
    return jnp.where(leak < 0.5, series, 1.0 - jnp.exp(-leak))


def split(x):
    high = x.astype(BF16)
    low = (x - high.astype(F32)).astype(BF16)
    return high, low


def exchange_kernel(
    count, near, start_ref, lists_hbm, x_hbm, leak_hbm, live_hbm, coef_hbm, delays_hbm, hilbert_hbm,
    packs_ref, inc_ref, toep_ref, hot_ref, chosen_ref, pick_ref, hilbert_ref,
    lists_ref, x_ref, leak_ref, live_ref, coef_ref, delays_ref,
    pack, packs, msg, msgs, delt, local, s1, r1, s2, r2,
):
    loads = [
        pltpu.make_async_copy(src, dst, local.at[n])
        for n, (src, dst) in enumerate(
            [
                (x_hbm, x_ref),
                (leak_hbm, leak_ref),
                (live_hbm, live_ref),
                (coef_hbm, coef_ref),
                (delays_hbm, delays_ref),
                (lists_hbm, lists_ref),
                (hilbert_hbm, hilbert_ref),
            ]
        )
    ]
    for load in loads:
        load.start()
    chans, samples = x_ref.shape
    passes, slots = lists_ref.shape
    bands = leak_ref.shape[0]
    slow, aperture = delays_ref.shape
    me = lax.axis_index("chan")
    barrier = pltpu.get_barrier_semaphore()
    for i in range(1, count):
        pl.semaphore_signal(
            barrier, inc=1, device_id={"chan": lax.rem(me + i, count)}, device_id_type=MESH
        )

    for load in loads[:3]:
        load.wait()
    lane = lax.broadcasted_iota(jnp.int32, (bands, chans), 1)
    live = jnp.broadcast_to(live_ref[...], (bands, chans)).astype(F32)
    pack[0:samples, :] = x_ref[...].astype(F32).T.astype(BF16)
    pack[samples : samples + bands, :] = leak_ref[...]
    pack[samples + bands : samples + 2 * bands, :] = live.astype(BF16)

    leak = leak_ref[...].astype(F32)
    inside = lane < start_ref[0] - me * chans
    leak_loc = jnp.where(inside, leak, 0.0)
    later = jnp.where(
        lax.broadcasted_iota(jnp.int32, (chans, chans), 0)
        > lax.broadcasted_iota(jnp.int32, (chans, chans), 1),
        1.0,
        0.0,
    ).astype(BF16)
    suffix = jnp.dot(
        jnp.concatenate([leak, leak_loc], axis=0).astype(BF16), later, preferred_element_type=F32
    )
    gain = inflow_of(leak) * live
    weights = jnp.concatenate([gain, jnp.where(inside, gain, 0.0)], axis=0) * jnp.exp(-suffix)
    high, low = split(weights)
    ends = jnp.dot(jnp.concatenate([high, low], axis=0), x_ref[...], preferred_element_type=F32)
    ends = ends[: 2 * bands] + ends[2 * bands :]
    total = jnp.broadcast_to(jnp.exp(-jnp.sum(leak, axis=1, keepdims=True)), (bands, chans))
    total_loc = jnp.exp(-jnp.sum(leak_loc, axis=1, keepdims=True))
    half = bands // 2
    msg[0:bands, :] = ends[:bands]
    msg[bands : bands + half, :] = jnp.where(lane[:half] < chans // 2, total[:half], total[half:])

    pl.semaphore_wait(barrier, count - 1)
    sends = []
    for i in range(1, count):
        sends.append(
            (
                pltpu.make_async_remote_copy(
                    src_ref=msg,
                    dst_ref=msgs.at[me],
                    send_sem=s1.at[i],
                    recv_sem=r1.at[i],
                    device_id={"chan": lax.rem(me + i, count)},
                    device_id_type=MESH,
                ),
                me + i < count,
                me - i >= 0,
            )
        )
        if i <= near:
            sends.append(
                (
                    pltpu.make_async_remote_copy(
                        src_ref=pack,
                        dst_ref=packs.at[i - 1],
                        send_sem=s2.at[i],
                        recv_sem=r2.at[i],
                        device_id={"chan": lax.rem(me + count - i, count)},
                        device_id_type=MESH,
                    ),
                    me - i >= 0,
                    me + i < count,
                )
            )
    for copy, sending, _ in sends:
        pl.when(sending)(copy.start)

    for load in loads[3:]:
        load.wait()
    eye = lax.broadcasted_iota(jnp.int32, (bands, bands), 0) == lax.broadcasted_iota(
        jnp.int32, (bands, bands), 1
    )
    b0, b1, b2, a1, a2 = [
        jnp.sum(jnp.where(eye, coef_ref[i : i + 1, :], 0.0), axis=1, keepdims=True) for i in range(5)
    ]
    last = samples - 1
    time = last - lax.broadcasted_iota(jnp.int32, (bands, samples), 1)

    def delayed(v, n):
        return jnp.where(time >= n, pltpu.roll(v, samples - n, 1), 0.0)

    resp = jnp.where(time == 0, 1.0, 0.0)
    before = jnp.zeros((bands, 1), F32)
    size = 1
    while size < samples:
        newest = resp[:, samples - size : samples - size + 1]
        following = -a1 * newest - a2 * before
        grown = following * resp - a2 * newest * delayed(resp, 1)
        resp = jnp.where(time < size, resp, delayed(grown, size))
        before = resp[:, samples - 2 * size + 1 : samples - 2 * size + 2]
        size *= 2
    resp = b0 * resp + b1 * delayed(resp, 1) + b2 * delayed(resp, 2)

    def toep_row(t, _):
        row = jnp.where(last - time <= t, pltpu.roll(resp, t + 1, 1), 0.0)
        high, low = split(row)
        at = pl.ds(pl.multiple_of(t * bands, bands), bands)
        toep_ref[at, 0:samples] = high
        toep_ref[at, samples : 2 * samples] = low
        return 0

    lax.fori_loop(0, samples, toep_row, 0, unroll=8)

    slow_id = lax.broadcasted_iota(jnp.int32, (1, slow), 1)
    for i in range(passes):
        for r in range(slots):
            n = i * slots + r
            chosen_ref[n : n + 1, :] = delays_ref[pl.ds(lists_ref[i, r], 1), :]
    pick_ref[...] = jnp.concatenate(
        [jnp.where(slow_id == lists_ref[0, r], 1.0, 0.0) for r in range(slots)], axis=0
    )
    delt[...] = delays_ref[...].T

    def hot_rows(d, _):
        at = pl.ds(pl.multiple_of(d * aperture, aperture), aperture)
        hot_ref[at, :] = jnp.where(delt[...] == d, 1.0, 0.0).astype(BF16)
        return 0

    lax.fori_loop(0, DMAX, hot_rows, 0)

    packs_ref[0] = pack[...]
    for copy, sending, receiving in sends:
        pl.when(sending)(copy.wait_send)
        pl.when(receiving)(copy.wait_recv)
    for i in range(1, near + 1):

        @pl.when(me + i < count)
        def _(i=i):
            packs_ref[i] = packs[i - 1]

        @pl.when(me + i >= count)
        def _(i=i):
            packs_ref[i] = jnp.zeros(packs_ref.shape[1:], BF16)

    def add_device(i, state):
        tile = msgs[i, bands : bands + half, :]
        keep = jnp.concatenate([tile[:, 0:1], tile[:, chans // 2 : chans // 2 + 1]], axis=0)
        return keep * state + msgs[i, 0:bands, :]

    incoming = lax.fori_loop(0, me, add_device, jnp.zeros((bands, samples), F32))
    inc_ref[...] = total_loc * incoming + ends[bands:]


def main_kernel(
    dims, start_ref, packs_ref, inc_ref, toep_ref, hot_ref, chosen_ref, pick_ref, hilbert_ref,
    out_hbm, out2_ref, xt, stacked, acc, acc2, power, power2, out_ref, sems,
):
    samples, bands, chans, passes = dims
    slow = hot_ref.shape[1]
    total, aperture = chosen_ref.shape
    slots = total // passes
    blocks = aperture // chans
    offset = lax.rem(start_ref[0], chans)
    points = samples * bands
    lead = (DMAX - 1) * bands

    rows = packs_ref.shape[1]
    lane = lax.broadcasted_iota(jnp.int32, (rows, chans), 1)
    turned = [pltpu.roll(packs_ref[j].astype(F32), chans - offset, 1) for j in range(blocks + 1)]
    window = [
        jnp.where(lane < chans - offset, turned[j], turned[j + 1]) for j in range(blocks)
    ]
    ones = lax.broadcasted_iota(jnp.int32, (chans, chans), 0) <= lax.broadcasted_iota(
        jnp.int32, (chans, chans), 1
    )
    tri = jnp.where(ones, 1.0, 0.0).astype(BF16)
    rise, fall, decay, live = [], [], [], []
    for j in range(blocks):
        leak = window[j][samples : samples + bands]
        live.append(window[j][samples + bands :])
        summed = jnp.dot(leak.astype(BF16), tri, preferred_element_type=F32)
        middle = 0.5 * summed[:, chans - 1 : chans]
        rise.append(jnp.exp(summed - middle) * inflow_of(leak))
        fall.append(jnp.exp(middle - summed))
        decay.append(jnp.exp(-summed))
    alive = jnp.concatenate(
        [window[j][:samples] * live[j][0:1, :] for j in range(blocks)], axis=1
    ).astype(BF16)
    stacked[0:samples, :] = alive
    stacked[samples : 2 * samples, :] = alive
    incoming = inc_ref[...]
    tri_wide = jnp.concatenate(
        [
            jnp.concatenate([tri, jnp.zeros_like(tri)], axis=1),
            jnp.concatenate([jnp.zeros_like(tri), tri], axis=1),
        ],
        axis=0,
    )
    xt[0:lead, :] = jnp.zeros((lead, aperture), BF16)
    tile = DMAX
    rising = jnp.concatenate(rise, axis=1)

    def filter_tile(i, energy, snaps):
        at = i * (tile * bands)
        taps = toep_ref[at : at + tile * bands, :]
        filtered = jnp.dot(taps, stacked[...], preferred_element_type=F32)
        filtered = filtered.astype(BF16).astype(F32)
        lifted = (filtered * jnp.concatenate([rising] * tile, axis=0)).astype(BF16)
        wide = 2 * chans
        sums = [
            jnp.dot(lifted[:, n * wide : (n + 1) * wide], tri_wide, preferred_element_type=F32)
            for n in range(blocks // 2)
        ]
        taps = taps[:, :samples].astype(F32) + taps[:, samples:].astype(F32)
        energy = list(energy)
        for k in range(tile):
            part = slice(k * bands, (k + 1) * bands)
            carry = jnp.broadcast_to(
                jnp.sum(taps[part] * incoming, axis=1, keepdims=True), (bands, chans)
            )
            row = slice(lead + at + k * bands, lead + at + (k + 1) * bands)
            for j in range(blocks):
                cols = slice(j * chans, (j + 1) * chans)
                inner = (j % 2) * chans
                mean = fall[j] * sums[j // 2][part, inner : inner + chans] + decay[j] * carry
                if j + 1 < blocks:
                    carry = jnp.broadcast_to(mean[:, chans - 1 : chans], (bands, chans))
                d = (live[j] * (filtered[part, cols] - mean)).astype(BF16)
                xt[row, cols] = d
                d = d.astype(F32)
                energy[j] = energy[j] + d * d
            if i == samples // tile - 1:
                snaps.append(
                    jnp.concatenate([jnp.sum(e, axis=0, keepdims=True) for e in energy], axis=1)
                )
        return tuple(energy)

    energy = tuple(jnp.zeros((bands, chans), F32) for _ in range(blocks))
    snaps = []
    for i in range(samples // tile):
        energy = filter_tile(i, energy, snaps)
    norms = snaps[::-1]

    step = points // 2
    tiles = slow // LANES
    scale = 1.0 / math.sqrt(aperture)

    def stack(i, _):
        at = pl.multiple_of(i * step, step)
        lagged = jnp.concatenate(
            [
                xt[pl.ds(pl.multiple_of(at + (DMAX - 1 - d) * bands, bands), step), :]
                for d in range(DMAX)
            ],
            axis=1,
        )
        beams = jnp.dot(lagged, hot_ref[...], preferred_element_type=F32) * scale
        for j in range(tiles):
            acc[j, pl.ds(at, step), :] = beams[:, j * LANES : (j + 1) * LANES]
        return 0

    lax.fori_loop(0, points // step, stack, 0)

    def power_of(s):
        turned = jnp.dot(hilbert_ref[...], s.astype(BF16), preferred_element_type=F32)
        return (s * s + turned * turned).T

    def refine():
        pad = jnp.zeros((slots, DMAX * bands), F32)
        length = points + DMAX * bands
        beams = jnp.concatenate([acc[j].astype(BF16) for j in range(tiles)], axis=1)
        guide = lax.dot_general(
            pick_ref[...].astype(BF16), beams, NT_DIMS, preferred_element_type=F32
        )
        mask = jnp.concatenate([v[0:1, :] for v in live], axis=1)
        results = []
        for i in range(passes):
            chosen = chosen_ref[i * slots : (i + 1) * slots, :]
            guide = guide.astype(BF16).astype(F32)
            padded = jnp.concatenate([guide, pad], axis=1)
            shifted = [padded[:, :points]] + [
                pltpu.roll(padded, length - d * bands, 1)[:, :points] for d in range(1, DMAX)
            ]
            shifted = jnp.concatenate(shifted, axis=0).astype(BF16)
            products = jnp.dot(shifted, xt[lead : lead + points, :], preferred_element_type=F32)
            numerator = jnp.zeros((slots, aperture), F32)
            strength = jnp.zeros((slots, aperture), F32)
            for d in range(DMAX):
                match = chosen == d
                numerator = numerator + jnp.where(
                    match, products[d * slots : (d + 1) * slots, :], 0.0
                )
                strength = strength + jnp.where(match, norms[d], 0.0)
            guide_norm = jnp.sqrt(jnp.sum(guide * guide, axis=1, keepdims=True) + EPS)
            coherence = numerator / (jnp.sqrt(strength + EPS) * guide_norm)
            weight = mask * (0.25 + jnp.maximum(coherence, 0.0))
            weight = weight.astype(BF16).astype(F32)
            spread = jnp.concatenate(
                [jnp.where(chosen == d, weight, 0.0) for d in range(DMAX)], axis=0
            ).astype(BF16)
            parts = lax.dot_general(
                spread, xt[lead : lead + points, :], NT_DIMS, preferred_element_type=F32
            )
            refined = parts[0:slots, :]
            for d in range(1, DMAX):
                part = jnp.concatenate([parts[d * slots : (d + 1) * slots, :], pad], axis=1)
                refined = refined + pltpu.roll(part, d * bands, 1)[:, :points]
            refined = refined / jnp.sqrt(1.0 + jnp.sum(weight * weight, axis=1, keepdims=True))
            results.append(refined)
            guide = refined
        results.append(jnp.zeros((LANES - total, points), F32))
        acc2[...] = jnp.concatenate(results, axis=0).T

    def envelopes():
        for band in range(bands):
            s = jnp.concatenate(
                [acc.at[j][pl.ds(band, samples, stride=bands), :] for j in range(tiles)], axis=1
            )
            power[pl.ds(band, slow, stride=bands), :] = power_of(s)

    envelopes()
    out_ref[...] = power[...].astype(BF16)
    send = pltpu.make_async_copy(out_ref, out_hbm, sems.at[0])
    send.start()
    refine()
    for band in range(bands):
        s = acc2[pl.ds(band, samples, stride=bands), :]
        power2[pl.ds(band, total, stride=bands), :] = power_of(s)[:total]
    out2_ref[...] = power2[...].astype(BF16)
    send.wait()


def per_device(traces, filter_coefs, leakage, live_mask, aperture_starts, delays, refine_lists):
    chans, samples = traces.shape
    bands = filter_coefs.shape[0]
    slow, aperture = delays.shape
    near = (aperture + chans - 1) // chans
    count = lax.axis_size("chan")
    passes, slots = refine_lists.shape[1:]
    points = samples * bands
    rows = samples + 2 * bands
    dma = pltpu.SemaphoreType.DMA
    total = passes * slots
    packs, inc, toep, hot, chosen, pick, hilbert = pl.pallas_call(
        functools.partial(exchange_kernel, count, near),
        out_shape=(
            jax.ShapeDtypeStruct((near + 1, rows, chans), BF16),
            jax.ShapeDtypeStruct((bands, samples), F32),
            jax.ShapeDtypeStruct((points, 2 * samples), BF16),
            jax.ShapeDtypeStruct((DMAX * aperture, slow), BF16),
            jax.ShapeDtypeStruct((total, aperture), jnp.int32),
            jax.ShapeDtypeStruct((slots, slow), F32),
            jax.ShapeDtypeStruct((samples, samples), BF16),
        ),
        in_specs=[SM] + [HB] * 7,
        out_specs=(VM,) * 7,
        scratch_shapes=[
            pltpu.SMEM((passes, slots), jnp.int32),
            pltpu.VMEM((chans, samples), BF16),
            pltpu.VMEM((bands, chans), BF16),
            pltpu.VMEM((1, chans), jnp.int32),
            pltpu.VMEM((5, bands), F32),
            pltpu.VMEM((slow, aperture), jnp.int32),
            pltpu.VMEM((rows, chans), BF16),
            pltpu.VMEM((near, rows, chans), BF16),
            pltpu.VMEM((bands + bands // 2, samples), F32),
            pltpu.VMEM((count, bands + bands // 2, samples), F32),
            pltpu.VMEM((aperture, slow), jnp.int32),
            dma((7,)), dma((count,)), dma((count,)), dma((near + 1,)), dma((near + 1,)),
        ],
        compiler_params=pltpu.CompilerParams(
            collective_id=0, has_side_effects=True, vmem_limit_bytes=14 * MIB
        ),
    )(
        aperture_starts,
        *[
            pltpu.with_memory_space_constraint(v, pltpu.HBM)
            for v in (
                refine_lists[0], traces, leakage.T, live_mask[None, :], filter_coefs.T, delays,
                hilbert_table(samples),
            )
        ],
    )
    beam, refined = pl.pallas_call(
        functools.partial(main_kernel, (samples, bands, chans, passes)),
        out_shape=(
            jax.ShapeDtypeStruct((slow * bands, samples), BF16),
            jax.ShapeDtypeStruct((total * bands, samples), BF16),
        ),
        in_specs=[SM] + [VM] * 7,
        out_specs=(HB, VM),
        scratch_shapes=[
            pltpu.VMEM((points + (DMAX - 1) * bands, aperture), BF16),
            pltpu.VMEM((2 * samples, aperture), BF16),
            pltpu.VMEM((slow // LANES, points, LANES), F32),
            pltpu.VMEM((points, LANES), F32),
            pltpu.VMEM((slow * bands, samples), F32),
            pltpu.VMEM((total * bands, samples), F32),
            pltpu.VMEM((slow * bands, samples), BF16),
            dma((1,)),
        ],
        compiler_params=pltpu.CompilerParams(vmem_limit_bytes=32 * MIB),
    )(aperture_starts, packs, inc, toep, hot, chosen, pick, hilbert)
    return (
        beam.reshape(1, slow, bands, samples),
        refined.reshape(1, passes, slots, bands, samples),
    )


def solution(mesh):
    return jax.shard_map(
        per_device,
        mesh=mesh,
        in_specs=(
            P(("cables", "chan"), None),
            P(),
            P(("cables", "chan"), None),
            P(("cables", "chan")),
            P(("cables", "chan")),
            P(),
            P(("cables", "chan"), None, None),
        ),
        out_specs=(
            P(("cables", "chan"), None, None, None),
            P(("cables", "chan"), None, None, None, None),
        ),
        check_vma=False,
    )
```

```python
import functools
import math

import numpy as np

import jax
import jax.numpy as jnp
from jax import lax
from jax.experimental import pallas as pl
from jax.experimental.pallas import tpu as pltpu
from jax.sharding import PartitionSpec as P

DMAX = 16
LANES = 128
EPS = 1e-06
MIB = 1024 * 1024
MESH = pl.DeviceIdType.MESH
VM = pl.BlockSpec(memory_space=pltpu.VMEM)
SM = pl.BlockSpec(memory_space=pltpu.SMEM)
HB = pl.BlockSpec(memory_space=pltpu.HBM)
F32 = jnp.float32
BF16 = jnp.bfloat16
NT_DIMS = (((1,), (1,)), ((), ()))


def hilbert_table(samples):
    index = np.arange(samples)
    offset = (index[:, None] - index[None, :]) % samples
    odd = offset % 2 == 1
    phase = np.pi * offset / samples
    table = np.where(odd, 2.0 / samples * np.cos(phase) / np.where(odd, np.sin(phase), 1.0), 0.0)
    return jnp.asarray(table.astype(np.float32).astype(jnp.bfloat16))


def inflow_of(leak):
    series = leak * (1.0 - leak * (0.5 - leak * (1.0 / 6.0 - leak * (1.0 / 24.0 - leak * (
        1.0 / 120.0 - leak * (1.0 / 720.0 - leak * (1.0 / 5040.0)))))))
    return jnp.where(leak < 0.5, series, 1.0 - jnp.exp(-leak))


def split(x):
    high = x.astype(BF16)
    low = (x - high.astype(F32)).astype(BF16)
    return high, low


def exchange_kernel(
    count, near, start_ref, lists_hbm, x_hbm, leak_hbm, live_hbm, coef_hbm, delays_hbm, hilbert_hbm,
    packs_ref, inc_ref, toep_ref, hot_ref, chosen_ref, pick_ref, hilbert_ref,
    lists_ref, x_ref, leak_ref, live_ref, coef_ref, delays_ref,
    pack, packs, msg, msgs, delt, local, s1, r1, s2, r2,
):
    loads = [
        pltpu.make_async_copy(src, dst, local.at[n])
        for n, (src, dst) in enumerate(
            [
                (x_hbm, x_ref),
                (leak_hbm, leak_ref),
                (live_hbm, live_ref),
                (coef_hbm, coef_ref),
                (delays_hbm, delays_ref),
                (lists_hbm, lists_ref),
                (hilbert_hbm, hilbert_ref),
            ]
        )
    ]
    for load in loads:
        load.start()
    chans, samples = x_ref.shape
    passes, slots = lists_ref.shape
    bands = leak_ref.shape[0]
    slow, aperture = delays_ref.shape
    me = lax.axis_index("chan")
    barrier = pltpu.get_barrier_semaphore()
    for i in range(1, count):
        pl.semaphore_signal(
            barrier, inc=1, device_id={"chan": lax.rem(me + i, count)}, device_id_type=MESH
        )

    for load in loads[:3]:
        load.wait()
    lane = lax.broadcasted_iota(jnp.int32, (bands, chans), 1)
    live = jnp.broadcast_to(live_ref[...], (bands, chans)).astype(F32)
    pack[0:samples, :] = x_ref[...].astype(F32).T.astype(BF16)
    pack[samples : samples + bands, :] = leak_ref[...]
    pack[samples + bands : samples + 2 * bands, :] = live.astype(BF16)

    leak = leak_ref[...].astype(F32)
    inside = lane < start_ref[0] - me * chans
    leak_loc = jnp.where(inside, leak, 0.0)
    later = jnp.where(
        lax.broadcasted_iota(jnp.int32, (chans, chans), 0)
        > lax.broadcasted_iota(jnp.int32, (chans, chans), 1),
        1.0,
        0.0,
    ).astype(BF16)
    suffix = jnp.dot(
        jnp.concatenate([leak, leak_loc], axis=0).astype(BF16), later, preferred_element_type=F32
    )
    gain = inflow_of(leak) * live
    weights = jnp.concatenate([gain, jnp.where(inside, gain, 0.0)], axis=0) * jnp.exp(-suffix)
    high, low = split(weights)
    ends = jnp.dot(jnp.concatenate([high, low], axis=0), x_ref[...], preferred_element_type=F32)
    ends = ends[: 2 * bands] + ends[2 * bands :]
    total = jnp.broadcast_to(jnp.exp(-jnp.sum(leak, axis=1, keepdims=True)), (bands, chans))
    total_loc = jnp.exp(-jnp.sum(leak_loc, axis=1, keepdims=True))
    half = bands // 2
    msg[0:bands, :] = ends[:bands]
    msg[bands : bands + half, :] = jnp.where(lane[:half] < chans // 2, total[:half], total[half:])

    pl.semaphore_wait(barrier, count - 1)
    sends = []
    for i in range(1, count):
        sends.append(
            (
                pltpu.make_async_remote_copy(
                    src_ref=msg,
                    dst_ref=msgs.at[me],
                    send_sem=s1.at[i],
                    recv_sem=r1.at[i],
                    device_id={"chan": lax.rem(me + i, count)},
                    device_id_type=MESH,
                ),
                me + i < count,
                me - i >= 0,
            )
        )
        if i <= near:
            sends.append(
                (
                    pltpu.make_async_remote_copy(
                        src_ref=pack,
                        dst_ref=packs.at[i - 1],
                        send_sem=s2.at[i],
                        recv_sem=r2.at[i],
                        device_id={"chan": lax.rem(me + count - i, count)},
                        device_id_type=MESH,
                    ),
                    me - i >= 0,
                    me + i < count,
                )
            )
    for copy, sending, _ in sends:
        pl.when(sending)(copy.start)

    for load in loads[3:]:
        load.wait()
    eye = lax.broadcasted_iota(jnp.int32, (bands, bands), 0) == lax.broadcasted_iota(
        jnp.int32, (bands, bands), 1
    )
    b0, b1, b2, a1, a2 = [
        jnp.sum(jnp.where(eye, coef_ref[i : i + 1, :], 0.0), axis=1, keepdims=True) for i in range(5)
    ]
    last = samples - 1
    time = last - lax.broadcasted_iota(jnp.int32, (bands, samples), 1)

    def delayed(v, n):
        return jnp.where(time >= n, pltpu.roll(v, samples - n, 1), 0.0)

    resp = jnp.where(time == 0, 1.0, 0.0)
    before = jnp.zeros((bands, 1), F32)
    size = 1
    while size < samples:
        newest = resp[:, samples - size : samples - size + 1]
        following = -a1 * newest - a2 * before
        grown = following * resp - a2 * newest * delayed(resp, 1)
        resp = jnp.where(time < size, resp, delayed(grown, size))
        before = resp[:, samples - 2 * size + 1 : samples - 2 * size + 2]
        size *= 2
    resp = b0 * resp + b1 * delayed(resp, 1) + b2 * delayed(resp, 2)

    def toep_row(t, _):
        row = jnp.where(last - time <= t, pltpu.roll(resp, t + 1, 1), 0.0)
        high, low = split(row)
        at = pl.ds(pl.multiple_of(t * bands, bands), bands)
        toep_ref[at, 0:samples] = high
        toep_ref[at, samples : 2 * samples] = low
        return 0

    lax.fori_loop(0, samples, toep_row, 0, unroll=8)

    slow_id = lax.broadcasted_iota(jnp.int32, (1, slow), 1)
    for i in range(passes):
        for r in range(slots):
            n = i * slots + r
            chosen_ref[n : n + 1, :] = delays_ref[pl.ds(lists_ref[i, r], 1), :]
    pick_ref[...] = jnp.concatenate(
        [jnp.where(slow_id == lists_ref[0, r], 1.0, 0.0) for r in range(slots)], axis=0
    )
    delt[...] = delays_ref[...].T

    def hot_rows(d, _):
        at = pl.ds(pl.multiple_of(d * aperture, aperture), aperture)
        hot_ref[at, :] = jnp.where(delt[...] == d, 1.0, 0.0).astype(BF16)
        return 0

    lax.fori_loop(0, DMAX, hot_rows, 0)

    packs_ref[0] = pack[...]
    for copy, sending, receiving in sends:
        pl.when(sending)(copy.wait_send)
        pl.when(receiving)(copy.wait_recv)
    for i in range(1, near + 1):

        @pl.when(me + i < count)
        def _(i=i):
            packs_ref[i] = packs[i - 1]

        @pl.when(me + i >= count)
        def _(i=i):
            packs_ref[i] = jnp.zeros(packs_ref.shape[1:], BF16)

    def add_device(i, state):
        tile = msgs[i, bands : bands + half, :]
        keep = jnp.concatenate([tile[:, 0:1], tile[:, chans // 2 : chans // 2 + 1]], axis=0)
        return keep * state + msgs[i, 0:bands, :]

    incoming = lax.fori_loop(0, me, add_device, jnp.zeros((bands, samples), F32))
    inc_ref[...] = total_loc * incoming + ends[bands:]


def main_kernel(
    dims, start_ref, packs_ref, inc_ref, toep_ref, hot_ref, chosen_ref, pick_ref, hilbert_ref,
    out_hbm, out2_ref, xt, stacked, lifted, acc, acc2, power, power2, out_ref, sems,
):
    samples, bands, chans, passes = dims
    slow = hot_ref.shape[1]
    total, aperture = chosen_ref.shape
    slots = total // passes
    blocks = aperture // chans
    offset = lax.rem(start_ref[0], chans)
    points = samples * bands
    lead = (DMAX - 1) * bands

    rows = packs_ref.shape[1]
    lane = lax.broadcasted_iota(jnp.int32, (rows, chans), 1)
    turned = [pltpu.roll(packs_ref[j].astype(F32), chans - offset, 1) for j in range(blocks + 1)]
    window = [
        jnp.where(lane < chans - offset, turned[j], turned[j + 1]) for j in range(blocks)
    ]
    ones = lax.broadcasted_iota(jnp.int32, (chans, chans), 0) <= lax.broadcasted_iota(
        jnp.int32, (chans, chans), 1
    )
    tri = jnp.where(ones, 1.0, 0.0).astype(BF16)
    rise, fall, live, carries = [], [], [], []
    carry = inc_ref[...]
    for j in range(blocks):
        leak = window[j][samples : samples + bands]
        live.append(window[j][samples + bands :])
        alive = (window[j][:samples] * live[j][0:1, :]).astype(BF16)
        stacked[0:samples, j * chans : (j + 1) * chans] = alive
        stacked[samples : 2 * samples, j * chans : (j + 1) * chans] = alive
        summed = jnp.dot(leak.astype(BF16), tri, preferred_element_type=F32)
        middle = 0.5 * summed[:, chans - 1 : chans]
        inflow = inflow_of(leak)
        rise.append(jnp.exp(summed - middle) * inflow)
        fall.append(jnp.exp(middle - summed))
        carries.append(carry * jnp.exp(-middle))
        if j + 1 < blocks:
            high, low = split(jnp.exp(summed - 2.0 * middle) * inflow)
            ends = lax.dot_general(
                jnp.concatenate([high, low], axis=0), alive, NT_DIMS, preferred_element_type=F32
            )
            carry = jnp.exp(-2.0 * middle) * carry + (ends[:bands] + ends[bands:])
    rising = jnp.concatenate(rise, axis=1)
    falling = jnp.concatenate(fall, axis=1)
    living = jnp.concatenate(live, axis=1)

    high, low = split(jnp.concatenate(carries * 2, axis=0))
    twice = jnp.concatenate([high, high], axis=1)
    kinds = 2 * blocks * bands
    lane = lax.broadcasted_iota(jnp.int32, (bands, kinds), 1)
    own = lax.rem(lane, bands) == lax.broadcasted_iota(jnp.int32, (bands, kinds), 0)
    first = lane < blocks * bands

    def every_sample(v):
        return jnp.concatenate([v] * samples, axis=0)

    taps = toep_ref[...]
    filtered = jnp.dot(taps, stacked[...], preferred_element_type=F32).astype(BF16)
    xt[lead : lead + points, :] = filtered
    lifted[:, 0:aperture] = (filtered.astype(F32) * every_sample(rising)).astype(BF16)
    begin = lax.dot_general(taps, twice, NT_DIMS, preferred_element_type=F32)
    begin += lax.dot_general(taps[:, :samples], low, NT_DIMS, preferred_element_type=F32)
    begin = jnp.where(every_sample(own), begin, 0.0)
    high = begin.astype(BF16).astype(F32)
    lifted[:, aperture:] = jnp.where(every_sample(first), high, begin - high).astype(BF16)

    wide = 2 * chans
    kind = lax.broadcasted_iota(jnp.int32, (kinds, wide), 0)
    place = lax.broadcasted_iota(jnp.int32, (kinds, wide), 1)
    tri_wide = jnp.concatenate(
        [
            jnp.concatenate([tri, jnp.zeros_like(tri)], axis=1),
            jnp.concatenate([jnp.zeros_like(tri), tri], axis=1),
        ],
        axis=0,
    )
    sums_of = [
        jnp.concatenate(
            [
                tri_wide,
                jnp.where(
                    lax.rem(kind // bands, blocks) == 2 * n + place // chans, 1.0, 0.0
                ).astype(BF16),
            ],
            axis=0,
        )
        for n in range(blocks // 2)
    ]
    xt[0:lead, :] = jnp.zeros((lead, aperture), BF16)

    for n in range(blocks // 2):
        cols = slice(n * wide, (n + 1) * wide)
        sums = jnp.dot(
            jnp.concatenate([lifted[:, cols], lifted[:, aperture:]], axis=1),
            sums_of[n],
            preferred_element_type=F32,
        )
        filtered = xt[lead : lead + points, cols].astype(F32)
        d = every_sample(living[:, cols]) * (filtered - every_sample(falling[:, cols]) * sums)
        xt[lead : lead + points, cols] = d.astype(BF16)

    energy = 0.0 * living
    norms = []
    for t in range(samples):
        d = xt[lead + t * bands : lead + (t + 1) * bands, :].astype(F32)
        energy = energy + d * d
        if t >= samples - DMAX:
            norms.insert(0, jnp.sum(energy, axis=0, keepdims=True))

    step = points // 2
    tiles = slow // LANES
    scale = 1.0 / math.sqrt(aperture)

    def stack(i, _):
        at = pl.multiple_of(i * step, step)
        lagged = jnp.concatenate(
            [
                xt[pl.ds(pl.multiple_of(at + (DMAX - 1 - d) * bands, bands), step), :]
                for d in range(DMAX)
            ],
            axis=1,
        )
        beams = jnp.dot(lagged, hot_ref[...], preferred_element_type=F32) * scale
        for j in range(tiles):
            acc[j, pl.ds(at, step), :] = beams[:, j * LANES : (j + 1) * LANES]
        return 0

    lax.fori_loop(0, points // step, stack, 0)

    def power_of(s):
        turned = jnp.dot(hilbert_ref[...], s.astype(BF16), preferred_element_type=F32)
        return (s * s + turned * turned).T

    def refine():
        pad = jnp.zeros((slots, DMAX * bands), F32)
        length = points + DMAX * bands
        beams = jnp.concatenate([acc[j].astype(BF16) for j in range(tiles)], axis=1)
        guide = lax.dot_general(
            pick_ref[...].astype(BF16), beams, NT_DIMS, preferred_element_type=F32
        )
        mask = jnp.concatenate([v[0:1, :] for v in live], axis=1)
        results = []
        for i in range(passes):
            chosen = chosen_ref[i * slots : (i + 1) * slots, :]
            guide = guide.astype(BF16).astype(F32)
            padded = jnp.concatenate([guide, pad], axis=1)
            shifted = [padded[:, :points]] + [
                pltpu.roll(padded, length - d * bands, 1)[:, :points] for d in range(1, DMAX)
            ]
            shifted = jnp.concatenate(shifted, axis=0).astype(BF16)
            products = jnp.dot(shifted, xt[lead : lead + points, :], preferred_element_type=F32)
            numerator = jnp.zeros((slots, aperture), F32)
            strength = jnp.zeros((slots, aperture), F32)
            for d in range(DMAX):
                match = chosen == d
                numerator = numerator + jnp.where(
                    match, products[d * slots : (d + 1) * slots, :], 0.0
                )
                strength = strength + jnp.where(match, norms[d], 0.0)
            guide_norm = jnp.sqrt(jnp.sum(guide * guide, axis=1, keepdims=True) + EPS)
            coherence = numerator / (jnp.sqrt(strength + EPS) * guide_norm)
            weight = mask * (0.25 + jnp.maximum(coherence, 0.0))
            weight = weight.astype(BF16).astype(F32)
            spread = jnp.concatenate(
                [jnp.where(chosen == d, weight, 0.0) for d in range(DMAX)], axis=0
            ).astype(BF16)
            parts = lax.dot_general(
                spread, xt[lead : lead + points, :], NT_DIMS, preferred_element_type=F32
            )
            refined = parts[0:slots, :]
            for d in range(1, DMAX):
                part = jnp.concatenate([parts[d * slots : (d + 1) * slots, :], pad], axis=1)
                refined = refined + pltpu.roll(part, d * bands, 1)[:, :points]
            refined = refined / jnp.sqrt(1.0 + jnp.sum(weight * weight, axis=1, keepdims=True))
            results.append(refined)
            guide = refined
        results.append(jnp.zeros((LANES - total, points), F32))
        acc2[...] = jnp.concatenate(results, axis=0).T

    def envelope(band, _):
        s = jnp.concatenate(
            [acc.at[j][pl.ds(band, samples, stride=bands), :] for j in range(tiles)], axis=1
        )
        power[pl.ds(band, slow, stride=bands), :] = power_of(s)
        return 0

    lax.fori_loop(0, bands, envelope, 0, unroll=8)
    out_ref[...] = power[...].astype(BF16)
    send = pltpu.make_async_copy(out_ref, out_hbm, sems.at[0])
    send.start()
    refine()
    per = LANES // total
    groups = []
    for g in range(bands // per):
        group = acc2[pl.ds(g * per, samples, stride=bands), :]
        for n in range(1, per):
            group += pltpu.roll(acc2[pl.ds(g * per + n, samples, stride=bands), :], n * total, 1)
        groups.append(group)
    both = power_of(jnp.concatenate(groups, axis=1))
    for band in range(bands):
        power2[pl.ds(band, total, stride=bands), :] = both[band * total : (band + 1) * total]
    out2_ref[...] = power2[...].astype(BF16)
    send.wait()


def per_device(traces, filter_coefs, leakage, live_mask, aperture_starts, delays, refine_lists):
    chans, samples = traces.shape
    bands = filter_coefs.shape[0]
    slow, aperture = delays.shape
    near = (aperture + chans - 1) // chans
    count = lax.axis_size("chan")
    passes, slots = refine_lists.shape[1:]
    points = samples * bands
    rows = samples + 2 * bands
    dma = pltpu.SemaphoreType.DMA
    total = passes * slots
    packs, inc, toep, hot, chosen, pick, hilbert = pl.pallas_call(
        functools.partial(exchange_kernel, count, near),
        out_shape=(
            jax.ShapeDtypeStruct((near + 1, rows, chans), BF16),
            jax.ShapeDtypeStruct((bands, samples), F32),
            jax.ShapeDtypeStruct((points, 2 * samples), BF16),
            jax.ShapeDtypeStruct((DMAX * aperture, slow), BF16),
            jax.ShapeDtypeStruct((total, aperture), jnp.int32),
            jax.ShapeDtypeStruct((slots, slow), F32),
            jax.ShapeDtypeStruct((samples, samples), BF16),
        ),
        in_specs=[SM] + [HB] * 7,
        out_specs=(VM,) * 7,
        scratch_shapes=[
            pltpu.SMEM((passes, slots), jnp.int32),
            pltpu.VMEM((chans, samples), BF16),
            pltpu.VMEM((bands, chans), BF16),
            pltpu.VMEM((1, chans), jnp.int32),
            pltpu.VMEM((5, bands), F32),
            pltpu.VMEM((slow, aperture), jnp.int32),
            pltpu.VMEM((rows, chans), BF16),
            pltpu.VMEM((near, rows, chans), BF16),
            pltpu.VMEM((bands + bands // 2, samples), F32),
            pltpu.VMEM((count, bands + bands // 2, samples), F32),
            pltpu.VMEM((aperture, slow), jnp.int32),
            dma((7,)), dma((count,)), dma((count,)), dma((near + 1,)), dma((near + 1,)),
        ],
        compiler_params=pltpu.CompilerParams(
            collective_id=0, has_side_effects=True, vmem_limit_bytes=14 * MIB
        ),
    )(
        aperture_starts,
        *[
            pltpu.with_memory_space_constraint(v, pltpu.HBM)
            for v in (
                refine_lists[0], traces, leakage.T, live_mask[None, :], filter_coefs.T, delays,
                hilbert_table(samples),
            )
        ],
    )
    beam, refined = pl.pallas_call(
        functools.partial(main_kernel, (samples, bands, chans, passes)),
        out_shape=(
            jax.ShapeDtypeStruct((slow * bands, samples), BF16),
            jax.ShapeDtypeStruct((total * bands, samples), BF16),
        ),
        in_specs=[SM] + [VM] * 7,
        out_specs=(HB, VM),
        scratch_shapes=[
            pltpu.VMEM((points + (DMAX - 1) * bands, aperture), BF16),
            pltpu.VMEM((2 * samples, aperture), BF16),
            pltpu.VMEM((points, aperture + 2 * (aperture // chans) * bands), BF16),
            pltpu.VMEM((slow // LANES, points, LANES), F32),
            pltpu.VMEM((points, LANES), F32),
            pltpu.VMEM((slow * bands, samples), F32),
            pltpu.VMEM((total * bands, samples), F32),
            pltpu.VMEM((slow * bands, samples), BF16),
            dma((1,)),
        ],
        compiler_params=pltpu.CompilerParams(vmem_limit_bytes=32 * MIB),
    )(aperture_starts, packs, inc, toep, hot, chosen, pick, hilbert)
    return (
        beam.reshape(1, slow, bands, samples),
        refined.reshape(1, passes, slots, bands, samples),
    )


def solution(mesh):
    return jax.shard_map(
        per_device,
        mesh=mesh,
        in_specs=(
            P(("cables", "chan"), None),
            P(),
            P(("cables", "chan"), None),
            P(("cables", "chan")),
            P(("cables", "chan")),
            P(),
            P(("cables", "chan"), None, None),
        ),
        out_specs=(
            P(("cables", "chan"), None, None, None),
            P(("cables", "chan"), None, None, None, None),
        ),
        check_vma=False,
    )
```

```python
import functools
import math

import numpy as np

import jax
import jax.numpy as jnp
from jax import lax
from jax.experimental import pallas as pl
from jax.experimental.pallas import tpu as pltpu
from jax.sharding import PartitionSpec as P

DMAX = 16
LANES = 128
EPS = 1e-06
MIB = 1024 * 1024
MESH = pl.DeviceIdType.MESH
VM = pl.BlockSpec(memory_space=pltpu.VMEM)
SM = pl.BlockSpec(memory_space=pltpu.SMEM)
HB = pl.BlockSpec(memory_space=pltpu.HBM)
F32 = jnp.float32
BF16 = jnp.bfloat16
NT_DIMS = (((1,), (1,)), ((), ()))


def hilbert_table(samples):
    index = np.arange(samples)
    offset = (index[:, None] - index[None, :]) % samples
    odd = offset % 2 == 1
    phase = np.pi * offset / samples
    table = np.where(odd, 2.0 / samples * np.cos(phase) / np.where(odd, np.sin(phase), 1.0), 0.0)
    return jnp.asarray(table.astype(np.float32).astype(jnp.bfloat16))


def inflow_of(leak):
    series = leak * (1.0 - leak * (0.5 - leak * (1.0 / 6.0 - leak * (1.0 / 24.0 - leak * (
        1.0 / 120.0 - leak * (1.0 / 720.0 - leak * (1.0 / 5040.0)))))))
    return jnp.where(leak < 0.5, series, 1.0 - jnp.exp(-leak))


def split(x):
    high = x.astype(BF16)
    low = (x - high.astype(F32)).astype(BF16)
    return high, low


def exchange_kernel(
    count, near, start_ref, lists_hbm, x_hbm, leak_hbm, live_hbm, coef_hbm, delays_hbm, hilbert_hbm,
    packs_ref, inc_ref, toep_ref, hot_ref, chosen_ref, pick_ref, hilbert_ref,
    lists_ref, x_ref, leak_ref, live_ref, coef_ref, delays_ref,
    pack, packs, msg, msgs, delt, local, s1, r1, s2, r2,
):
    loads = [
        pltpu.make_async_copy(src, dst, local.at[n])
        for n, (src, dst) in enumerate(
            [
                (x_hbm, x_ref),
                (leak_hbm, leak_ref),
                (live_hbm, live_ref),
                (coef_hbm, coef_ref),
                (delays_hbm, delays_ref),
                (lists_hbm, lists_ref),
                (hilbert_hbm, hilbert_ref),
            ]
        )
    ]
    for load in loads:
        load.start()
    chans, samples = x_ref.shape
    passes, slots = lists_ref.shape
    bands = leak_ref.shape[0]
    slow, aperture = delays_ref.shape
    me = lax.axis_index("chan")
    barrier = pltpu.get_barrier_semaphore()
    for i in range(1, count):
        pl.semaphore_signal(
            barrier, inc=1, device_id={"chan": lax.rem(me + i, count)}, device_id_type=MESH
        )

    for load in loads[:3]:
        load.wait()
    lane = lax.broadcasted_iota(jnp.int32, (bands, chans), 1)
    live = jnp.broadcast_to(live_ref[...], (bands, chans)).astype(F32)
    pack[0:samples, :] = x_ref[...].astype(F32).T.astype(BF16)
    pack[samples : samples + bands, :] = leak_ref[...]
    pack[samples + bands : samples + 2 * bands, :] = live.astype(BF16)

    leak = leak_ref[...].astype(F32)
    inside = lane < start_ref[0] - me * chans
    leak_loc = jnp.where(inside, leak, 0.0)
    later = jnp.where(
        lax.broadcasted_iota(jnp.int32, (chans, chans), 0)
        > lax.broadcasted_iota(jnp.int32, (chans, chans), 1),
        1.0,
        0.0,
    ).astype(BF16)
    suffix = jnp.dot(
        jnp.concatenate([leak, leak_loc], axis=0).astype(BF16), later, preferred_element_type=F32
    )
    gain = inflow_of(leak) * live
    weights = jnp.concatenate([gain, jnp.where(inside, gain, 0.0)], axis=0) * jnp.exp(-suffix)
    high, low = split(weights)
    ends = jnp.dot(jnp.concatenate([high, low], axis=0), x_ref[...], preferred_element_type=F32)
    ends = ends[: 2 * bands] + ends[2 * bands :]
    total = jnp.broadcast_to(jnp.exp(-jnp.sum(leak, axis=1, keepdims=True)), (bands, chans))
    total_loc = jnp.exp(-jnp.sum(leak_loc, axis=1, keepdims=True))
    half = bands // 2
    msg[0:bands, :] = ends[:bands]
    msg[bands : bands + half, :] = jnp.where(lane[:half] < chans // 2, total[:half], total[half:])

    for i in range(count - 1):

        @pl.when(i >= me)
        def _(i=i):
            msgs[i, 0:bands, :] = jnp.zeros((bands, samples), F32)
            msgs[i, bands : bands + half, :] = jnp.ones((half, samples), F32)

    pl.semaphore_wait(barrier, count - 1)
    sends = []
    for i in [*range(1, near + 1)][::-1]:
        sends.append(
            (
                pltpu.make_async_remote_copy(
                    src_ref=pack,
                    dst_ref=packs.at[i - 1],
                    send_sem=s2.at[i],
                    recv_sem=r2.at[i],
                    device_id={"chan": lax.rem(me + count - i, count)},
                    device_id_type=MESH,
                ),
                me - i >= 0,
                me + i < count,
            )
        )
    for i in [*range(1, count)][::-1]:
        sends.append(
            (
                pltpu.make_async_remote_copy(
                    src_ref=msg,
                    dst_ref=msgs.at[me],
                    send_sem=s1.at[i],
                    recv_sem=r1.at[i],
                    device_id={"chan": lax.rem(me + i, count)},
                    device_id_type=MESH,
                ),
                me + i < count,
                me - i >= 0,
            )
        )
    for copy, sending, _ in sends:
        pl.when(sending)(copy.start)

    for load in loads[3:]:
        load.wait()
    eye = lax.broadcasted_iota(jnp.int32, (bands, bands), 0) == lax.broadcasted_iota(
        jnp.int32, (bands, bands), 1
    )
    b0, b1, b2, a1, a2 = [
        jnp.sum(jnp.where(eye, coef_ref[i : i + 1, :], 0.0), axis=1, keepdims=True) for i in range(5)
    ]
    last = samples - 1
    time = last - lax.broadcasted_iota(jnp.int32, (bands, samples), 1)

    def delayed(v, n):
        return jnp.where(time >= n, pltpu.roll(v, samples - n, 1), 0.0)

    resp = jnp.where(time == 0, 1.0, 0.0)
    before = jnp.zeros((bands, 1), F32)
    size = 1
    while size < samples:
        newest = resp[:, samples - size : samples - size + 1]
        following = -a1 * newest - a2 * before
        grown = following * resp - a2 * newest * delayed(resp, 1)
        resp = jnp.where(time < size, resp, delayed(grown, size))
        before = resp[:, samples - 2 * size + 1 : samples - 2 * size + 2]
        size *= 2
    resp = b0 * resp + b1 * delayed(resp, 1) + b2 * delayed(resp, 2)

    def toep_row(t, _):
        row = jnp.where(last - time <= t, pltpu.roll(resp, t + 1, 1), 0.0)
        high, low = split(row)
        at = pl.ds(pl.multiple_of(t * bands, bands), bands)
        toep_ref[at, 0:samples] = high
        toep_ref[at, samples : 2 * samples] = low
        return 0

    lax.fori_loop(0, samples, toep_row, 0, unroll=8)

    slow_id = lax.broadcasted_iota(jnp.int32, (1, slow), 1)
    for i in range(passes):
        for r in range(slots):
            n = i * slots + r
            chosen_ref[n : n + 1, :] = delays_ref[pl.ds(lists_ref[i, r], 1), :]
    pick_ref[...] = jnp.concatenate(
        [jnp.where(slow_id == lists_ref[0, r], 1.0, 0.0) for r in range(slots)], axis=0
    )
    delt[...] = delays_ref[...].T

    def hot_rows(q, _):
        at = pl.ds(pl.multiple_of(q * aperture, aperture), aperture)
        even = jnp.where(delt[...] == 2 * q, 1.0, 0.0)
        odd = jnp.where(delt[...] == 2 * q + 1, 1.0, 0.0)
        hot_ref[0, at, :] = even.astype(BF16)
        hot_ref[1, at, :] = odd.astype(BF16)
        hot_ref[2, at, :] = (even + odd).astype(BF16)
        return 0

    lax.fori_loop(0, DMAX // 2, hot_rows, 0)

    packs_ref[0] = pack[...]
    for copy, sending, receiving in sends:
        pl.when(sending)(copy.wait_send)
        pl.when(receiving)(copy.wait_recv)
    for i in range(1, near + 1):

        @pl.when(me + i < count)
        def _(i=i):
            packs_ref[i] = packs[i - 1]

        @pl.when(me + i >= count)
        def _(i=i):
            packs_ref[i] = jnp.zeros(packs_ref.shape[1:], BF16)

    incoming = jnp.zeros((bands, samples), F32)
    for i in range(count - 1):
        tile = msgs[i, bands : bands + half, :]
        keep = jnp.concatenate([tile[:, 0:1], tile[:, chans // 2 : chans // 2 + 1]], axis=0)
        incoming = keep * incoming + msgs[i, 0:bands, :]
    inc_ref[...] = total_loc * incoming + ends[bands:]


def main_kernel(
    dims, start_ref, packs_ref, inc_ref, toep_ref, hot_ref, chosen_ref, pick_ref, hilbert_ref,
    out_hbm, out2_ref, xt, phases, stacked, lifted, parts3, acc, acc2, power, power2, out_ref, sems,
):
    samples, bands, chans, passes = dims
    slow = hot_ref.shape[2]
    total, aperture = chosen_ref.shape
    slots = total // passes
    blocks = aperture // chans
    offset = lax.rem(start_ref[0], chans)
    points = samples * bands
    pairs = samples // 2
    lags = DMAX // 2

    rows = packs_ref.shape[1]
    lane = lax.broadcasted_iota(jnp.int32, (rows, chans), 1)
    turned = [pltpu.roll(packs_ref[j].astype(F32), chans - offset, 1) for j in range(blocks + 1)]
    window = [
        jnp.where(lane < chans - offset, turned[j], turned[j + 1]) for j in range(blocks)
    ]
    ones = lax.broadcasted_iota(jnp.int32, (chans, chans), 0) <= lax.broadcasted_iota(
        jnp.int32, (chans, chans), 1
    )
    tri = jnp.where(ones, 1.0, 0.0).astype(BF16)
    rise, fall, live, carries = [], [], [], []
    carry = inc_ref[...]
    for j in range(blocks):
        leak = window[j][samples : samples + bands]
        live.append(window[j][samples + bands :])
        alive = (window[j][:samples] * live[j][0:1, :]).astype(BF16)
        stacked[0:samples, j * chans : (j + 1) * chans] = alive
        stacked[samples : 2 * samples, j * chans : (j + 1) * chans] = alive
        summed = jnp.dot(leak.astype(BF16), tri, preferred_element_type=F32)
        middle = 0.5 * summed[:, chans - 1 : chans]
        inflow = inflow_of(leak)
        rise.append(jnp.exp(summed - middle) * inflow)
        fall.append(jnp.exp(middle - summed))
        carries.append(carry * jnp.exp(-middle))
        if j + 1 < blocks:
            high, low = split(jnp.exp(summed - 2.0 * middle) * inflow)
            ends = lax.dot_general(
                jnp.concatenate([high, low], axis=0), alive, NT_DIMS, preferred_element_type=F32
            )
            carry = jnp.exp(-2.0 * middle) * carry + (ends[:bands] + ends[bands:])
    rising = jnp.concatenate(rise, axis=1)
    falling = jnp.concatenate(fall, axis=1)
    living = jnp.concatenate(live, axis=1)

    high, low = split(jnp.concatenate(carries * 2, axis=0))
    twice = jnp.concatenate([high, high], axis=1)
    kinds = 2 * blocks * bands
    lane = lax.broadcasted_iota(jnp.int32, (bands, kinds), 1)
    own = lax.rem(lane, bands) == lax.broadcasted_iota(jnp.int32, (bands, kinds), 0)
    first = lane < blocks * bands

    def every_sample(v):
        return jnp.concatenate([v] * samples, axis=0)

    taps = toep_ref[...]
    filtered = jnp.dot(taps, stacked[...], preferred_element_type=F32).astype(BF16)
    xt[...] = filtered
    lifted[:, 0:aperture] = (filtered.astype(F32) * every_sample(rising)).astype(BF16)
    begin = lax.dot_general(taps, twice, NT_DIMS, preferred_element_type=F32)
    begin += lax.dot_general(taps[:, :samples], low, NT_DIMS, preferred_element_type=F32)
    begin = jnp.where(every_sample(own), begin, 0.0)
    high = begin.astype(BF16).astype(F32)
    lifted[:, aperture:] = jnp.where(every_sample(first), high, begin - high).astype(BF16)

    wide = 2 * chans
    kind = lax.broadcasted_iota(jnp.int32, (kinds, wide), 0)
    place = lax.broadcasted_iota(jnp.int32, (kinds, wide), 1)
    tri_wide = jnp.concatenate(
        [
            jnp.concatenate([tri, jnp.zeros_like(tri)], axis=1),
            jnp.concatenate([jnp.zeros_like(tri), tri], axis=1),
        ],
        axis=0,
    )
    sums_of = [
        jnp.concatenate(
            [
                tri_wide,
                jnp.where(
                    lax.rem(kind // bands, blocks) == 2 * n + place // chans, 1.0, 0.0
                ).astype(BF16),
            ],
            axis=0,
        )
        for n in range(blocks // 2)
    ]
    phases[:, 0:lags] = jnp.zeros((3, lags, bands, aperture), BF16)

    for n in range(blocks // 2):
        cols = slice(n * wide, (n + 1) * wide)
        sums = jnp.dot(
            jnp.concatenate([lifted[:, cols], lifted[:, aperture:]], axis=1),
            sums_of[n],
            preferred_element_type=F32,
        )
        filtered = xt[:, cols].astype(F32)
        d = every_sample(living[:, cols]) * (filtered - every_sample(falling[:, cols]) * sums)
        d = d.astype(BF16)
        xt[:, cols] = d
        d = d.reshape(pairs, 2, bands, wide)
        phases[0, lags:, :, cols] = d[:, 0]
        phases[1, lags:, :, cols] = d[:, 1]
        phases[2, lags:, :, cols] = (d[:, 0].astype(F32) + d[:, 1].astype(F32)).astype(BF16)

    energy = 0.0 * living
    norms = []
    for t in range(samples):
        d = xt[t * bands : (t + 1) * bands, :].astype(F32)
        energy = energy + d * d
        if t >= samples - DMAX:
            norms.insert(0, jnp.sum(energy, axis=0, keepdims=True))

    tiles = slow // LANES
    scale = 1.0 / math.sqrt(aperture)

    def stack(i, _):
        lagged = jnp.concatenate(
            [
                phases[i, lags - q : lags - q + pairs].reshape(pairs * bands, aperture)
                for q in range(lags)
            ],
            axis=1,
        )
        beams = jnp.dot(lagged, hot_ref[i], preferred_element_type=F32) * scale
        parts3[i, bands:, :] = beams
        return 0

    lax.fori_loop(0, 3, stack, 0)
    parts3[1, 0:bands, :] = jnp.zeros((bands, slow), F32)
    for j in range(tiles):
        cols = slice(j * LANES, (j + 1) * LANES)
        even = parts3[0, bands:, cols]
        acc[j, :, 0] = (even + parts3[1, : pairs * bands, cols]).reshape(pairs, bands, LANES)
        odd = parts3[2, bands:, cols] - even - parts3[1, bands:, cols]
        acc[j, :, 1] = odd.reshape(pairs, bands, LANES)
    acc = acc.reshape(tiles, points, LANES)

    def power_of(s):
        turned = jnp.dot(hilbert_ref[...], s.astype(BF16), preferred_element_type=F32)
        return (s * s + turned * turned).T

    def refine():
        pad = jnp.zeros((slots, DMAX * bands), F32)
        length = points + DMAX * bands
        beams = jnp.concatenate([acc[j].astype(BF16) for j in range(tiles)], axis=1)
        guide = lax.dot_general(
            pick_ref[...].astype(BF16), beams, NT_DIMS, preferred_element_type=F32
        )
        mask = jnp.concatenate([v[0:1, :] for v in live], axis=1)
        results = []
        for i in range(passes):
            chosen = chosen_ref[i * slots : (i + 1) * slots, :]
            guide = guide.astype(BF16).astype(F32)
            padded = jnp.concatenate([guide, pad], axis=1)
            shifted = [padded[:, :points]] + [
                pltpu.roll(padded, length - d * bands, 1)[:, :points] for d in range(1, DMAX)
            ]
            shifted = jnp.concatenate(shifted, axis=0).astype(BF16)
            products = jnp.dot(shifted, xt[...], preferred_element_type=F32)
            numerator = jnp.zeros((slots, aperture), F32)
            strength = jnp.zeros((slots, aperture), F32)
            for d in range(DMAX):
                match = chosen == d
                numerator = numerator + jnp.where(
                    match, products[d * slots : (d + 1) * slots, :], 0.0
                )
                strength = strength + jnp.where(match, norms[d], 0.0)
            guide_norm = jnp.sqrt(jnp.sum(guide * guide, axis=1, keepdims=True) + EPS)
            coherence = numerator / (jnp.sqrt(strength + EPS) * guide_norm)
            weight = mask * (0.25 + jnp.maximum(coherence, 0.0))
            weight = weight.astype(BF16).astype(F32)
            spread = jnp.concatenate(
                [jnp.where(chosen == d, weight, 0.0) for d in range(DMAX)], axis=0
            ).astype(BF16)
            parts = lax.dot_general(
                spread, xt[...], NT_DIMS, preferred_element_type=F32
            )
            refined = parts[0:slots, :]
            for d in range(1, DMAX):
                part = jnp.concatenate([parts[d * slots : (d + 1) * slots, :], pad], axis=1)
                refined = refined + pltpu.roll(part, d * bands, 1)[:, :points]
            refined = refined / jnp.sqrt(1.0 + jnp.sum(weight * weight, axis=1, keepdims=True))
            results.append(refined)
            guide = refined
        results.append(jnp.zeros((LANES - total, points), F32))
        acc2[...] = jnp.concatenate(results, axis=0).T

    def envelope(band, _):
        s = jnp.concatenate(
            [acc.at[j][pl.ds(band, samples, stride=bands), :] for j in range(tiles)], axis=1
        )
        power[pl.ds(band, slow, stride=bands), :] = power_of(s)
        return 0

    lax.fori_loop(0, bands, envelope, 0, unroll=8)
    out_ref[...] = power[...].astype(BF16)
    send = pltpu.make_async_copy(out_ref, out_hbm, sems.at[0])
    send.start()
    refine()
    per = LANES // total
    groups = []
    for g in range(bands // per):
        group = acc2[pl.ds(g * per, samples, stride=bands), :]
        for n in range(1, per):
            group += pltpu.roll(acc2[pl.ds(g * per + n, samples, stride=bands), :], n * total, 1)
        groups.append(group)
    both = power_of(jnp.concatenate(groups, axis=1))
    for band in range(bands):
        power2[pl.ds(band, total, stride=bands), :] = both[band * total : (band + 1) * total]
    out2_ref[...] = power2[...].astype(BF16)
    send.wait()


def per_device(traces, filter_coefs, leakage, live_mask, aperture_starts, delays, refine_lists):
    chans, samples = traces.shape
    bands = filter_coefs.shape[0]
    slow, aperture = delays.shape
    near = (aperture + chans - 1) // chans
    count = lax.axis_size("chan")
    passes, slots = refine_lists.shape[1:]
    points = samples * bands
    rows = samples + 2 * bands
    dma = pltpu.SemaphoreType.DMA
    total = passes * slots
    packs, inc, toep, hot, chosen, pick, hilbert = pl.pallas_call(
        functools.partial(exchange_kernel, count, near),
        out_shape=(
            jax.ShapeDtypeStruct((near + 1, rows, chans), BF16),
            jax.ShapeDtypeStruct((bands, samples), F32),
            jax.ShapeDtypeStruct((points, 2 * samples), BF16),
            jax.ShapeDtypeStruct((3, DMAX // 2 * aperture, slow), BF16),
            jax.ShapeDtypeStruct((total, aperture), jnp.int32),
            jax.ShapeDtypeStruct((slots, slow), F32),
            jax.ShapeDtypeStruct((samples, samples), BF16),
        ),
        in_specs=[SM] + [HB] * 7,
        out_specs=(VM,) * 7,
        scratch_shapes=[
            pltpu.SMEM((passes, slots), jnp.int32),
            pltpu.VMEM((chans, samples), BF16),
            pltpu.VMEM((bands, chans), BF16),
            pltpu.VMEM((1, chans), jnp.int32),
            pltpu.VMEM((5, bands), F32),
            pltpu.VMEM((slow, aperture), jnp.int32),
            pltpu.VMEM((rows, chans), BF16),
            pltpu.VMEM((near, rows, chans), BF16),
            pltpu.VMEM((bands + bands // 2, samples), F32),
            pltpu.VMEM((count, bands + bands // 2, samples), F32),
            pltpu.VMEM((aperture, slow), jnp.int32),
            dma((7,)), dma((count,)), dma((count,)), dma((near + 1,)), dma((near + 1,)),
        ],
        compiler_params=pltpu.CompilerParams(
            collective_id=0, has_side_effects=True, vmem_limit_bytes=14 * MIB
        ),
    )(
        aperture_starts,
        *[
            pltpu.with_memory_space_constraint(v, pltpu.HBM)
            for v in (
                refine_lists[0], traces, leakage.T, live_mask[None, :], filter_coefs.T, delays,
                hilbert_table(samples),
            )
        ],
    )
    beam, refined = pl.pallas_call(
        functools.partial(main_kernel, (samples, bands, chans, passes)),
        out_shape=(
            jax.ShapeDtypeStruct((slow * bands, samples), BF16),
            jax.ShapeDtypeStruct((total * bands, samples), BF16),
        ),
        in_specs=[SM] + [VM] * 7,
        out_specs=(HB, VM),
        scratch_shapes=[
            pltpu.VMEM((points, aperture), BF16),
            pltpu.VMEM((3, (samples + DMAX) // 2, bands, aperture), BF16),
            pltpu.VMEM((2 * samples, aperture), BF16),
            pltpu.VMEM((points, aperture + 2 * (aperture // chans) * bands), BF16),
            pltpu.VMEM((3, points // 2 + bands, slow), F32),
            pltpu.VMEM((slow // LANES, samples // 2, 2, bands, LANES), F32),
            pltpu.VMEM((points, LANES), F32),
            pltpu.VMEM((slow * bands, samples), F32),
            pltpu.VMEM((total * bands, samples), F32),
            pltpu.VMEM((slow * bands, samples), BF16),
            dma((1,)),
        ],
        compiler_params=pltpu.CompilerParams(vmem_limit_bytes=32 * MIB),
    )(aperture_starts, packs, inc, toep, hot, chosen, pick, hilbert)
    return (
        beam.reshape(1, slow, bands, samples),
        refined.reshape(1, passes, slots, bands, samples),
    )


def solution(mesh):
    return jax.shard_map(
        per_device,
        mesh=mesh,
        in_specs=(
            P(("cables", "chan"), None),
            P(),
            P(("cables", "chan"), None),
            P(("cables", "chan")),
            P(("cables", "chan")),
            P(),
            P(("cables", "chan"), None, None),
        ),
        out_specs=(
            P(("cables", "chan"), None, None, None),
            P(("cables", "chan"), None, None, None, None),
        ),
        check_vma=False,
    )
```

```python
import functools
import math

import numpy as np

import jax
import jax.numpy as jnp
from jax import lax
from jax.experimental import pallas as pl
from jax.experimental.pallas import tpu as pltpu
from jax.sharding import PartitionSpec as P

DMAX = 16
LANES = 128
EPS = 1e-06
MIB = 1024 * 1024
MESH = pl.DeviceIdType.MESH
VM = pl.BlockSpec(memory_space=pltpu.VMEM)
SM = pl.BlockSpec(memory_space=pltpu.SMEM)
HB = pl.BlockSpec(memory_space=pltpu.HBM)
F32 = jnp.float32
BF16 = jnp.bfloat16
NT_DIMS = (((1,), (1,)), ((), ()))


def hilbert_table(samples):
    index = np.arange(samples)
    offset = (index[:, None] - index[None, :]) % samples
    odd = offset % 2 == 1
    phase = np.pi * offset / samples
    table = np.where(odd, 2.0 / samples * np.cos(phase) / np.where(odd, np.sin(phase), 1.0), 0.0)
    return jnp.asarray(table.astype(np.float32).astype(jnp.bfloat16))


def inflow_of(leak):
    series = leak * (1.0 - leak * (0.5 - leak * (1.0 / 6.0 - leak * (1.0 / 24.0 - leak * (
        1.0 / 120.0 - leak * (1.0 / 720.0 - leak * (1.0 / 5040.0)))))))
    return jnp.where(leak < 0.5, series, 1.0 - jnp.exp(-leak))


def split(x):
    high = x.astype(BF16)
    low = (x - high.astype(F32)).astype(BF16)
    return high, low


def exchange_kernel(
    count, near, start_ref, lists_hbm, x_hbm, leak_hbm, live_hbm, coef_hbm, delays_hbm, hilbert_hbm,
    packs_ref, inc_ref, toep_ref, hot_ref, chosen_ref, pick_ref, hilbert_ref,
    lists_ref, x_ref, leak_ref, live_ref, coef_ref, delays_ref,
    pack, packs, msg, msgs, delt, local, s1, r1, s2, r2,
):
    loads = [
        pltpu.make_async_copy(src, dst, local.at[n])
        for n, (src, dst) in enumerate(
            [
                (x_hbm, x_ref),
                (leak_hbm, leak_ref),
                (live_hbm, live_ref),
                (coef_hbm, coef_ref),
                (delays_hbm, delays_ref),
                (lists_hbm, lists_ref),
                (hilbert_hbm, hilbert_ref),
            ]
        )
    ]
    for load in loads:
        load.start()
    chans, samples = x_ref.shape
    passes, slots = lists_ref.shape
    bands = leak_ref.shape[0]
    slow, aperture = delays_ref.shape
    me = lax.axis_index("chan")
    barrier = pltpu.get_barrier_semaphore()
    for i in range(1, count):
        pl.semaphore_signal(
            barrier, inc=1, device_id={"chan": lax.rem(me + i, count)}, device_id_type=MESH
        )

    for load in loads[:3]:
        load.wait()
    lane = lax.broadcasted_iota(jnp.int32, (bands, chans), 1)
    live = jnp.broadcast_to(live_ref[...], (bands, chans)).astype(F32)
    pack[0:samples, :] = x_ref[...].astype(F32).T.astype(BF16)
    pack[samples : samples + bands, :] = leak_ref[...]
    pack[samples + bands : samples + 2 * bands, :] = live.astype(BF16)

    leak = leak_ref[...].astype(F32)
    inside = lane < start_ref[0] - me * chans
    leak_loc = jnp.where(inside, leak, 0.0)
    later = jnp.where(
        lax.broadcasted_iota(jnp.int32, (chans, chans), 0)
        > lax.broadcasted_iota(jnp.int32, (chans, chans), 1),
        1.0,
        0.0,
    ).astype(BF16)
    suffix = jnp.dot(
        jnp.concatenate([leak, leak_loc], axis=0).astype(BF16), later, preferred_element_type=F32
    )
    gain = inflow_of(leak) * live
    weights = jnp.concatenate([gain, jnp.where(inside, gain, 0.0)], axis=0) * jnp.exp(-suffix)
    high, low = split(weights)
    ends = jnp.dot(jnp.concatenate([high, low], axis=0), x_ref[...], preferred_element_type=F32)
    ends = ends[: 2 * bands] + ends[2 * bands :]
    total = jnp.broadcast_to(jnp.exp(-jnp.sum(leak, axis=1, keepdims=True)), (bands, chans))
    total_loc = jnp.exp(-jnp.sum(leak_loc, axis=1, keepdims=True))
    half = bands // 2
    msg[0:bands, :] = ends[:bands]
    msg[bands : bands + half, :] = jnp.where(lane[:half] < chans // 2, total[:half], total[half:])

    for i in range(count - 1):

        @pl.when(i >= me)
        def _(i=i):
            msgs[i, 0:bands, :] = jnp.zeros((bands, samples), F32)
            msgs[i, bands : bands + half, :] = jnp.ones((half, samples), F32)

    loads[4].wait()
    delt[...] = delays_ref[...].T

    def hot_rows(q, _):
        at = pl.ds(pl.multiple_of(q * aperture, aperture), aperture)
        even = jnp.where(delt[...] == 2 * q, 1.0, 0.0)
        odd = jnp.where(delt[...] == 2 * q + 1, 1.0, 0.0)
        hot_ref[0, at, :] = even.astype(BF16)
        hot_ref[1, at, :] = odd.astype(BF16)
        hot_ref[2, at, :] = (even + odd).astype(BF16)
        return 0

    lax.fori_loop(0, DMAX // 2, hot_rows, 0)

    pl.semaphore_wait(barrier, count - 1)
    sends = []
    for i in [*range(1, near + 1)][::-1]:
        sends.append(
            (
                pltpu.make_async_remote_copy(
                    src_ref=pack,
                    dst_ref=packs.at[i - 1],
                    send_sem=s2.at[i],
                    recv_sem=r2.at[i],
                    device_id={"chan": lax.rem(me + count - i, count)},
                    device_id_type=MESH,
                ),
                me - i >= 0,
                me + i < count,
            )
        )
    for i in [*range(1, count)][::-1]:
        sends.append(
            (
                pltpu.make_async_remote_copy(
                    src_ref=msg,
                    dst_ref=msgs.at[me],
                    send_sem=s1.at[i],
                    recv_sem=r1.at[i],
                    device_id={"chan": lax.rem(me + i, count)},
                    device_id_type=MESH,
                ),
                me + i < count,
                me - i >= 0,
            )
        )
    for copy, sending, _ in sends:
        pl.when(sending)(copy.start)

    for load in (loads[3], loads[5], loads[6]):
        load.wait()
    eye = lax.broadcasted_iota(jnp.int32, (bands, bands), 0) == lax.broadcasted_iota(
        jnp.int32, (bands, bands), 1
    )
    b0, b1, b2, a1, a2 = [
        jnp.sum(jnp.where(eye, coef_ref[i : i + 1, :], 0.0), axis=1, keepdims=True) for i in range(5)
    ]
    last = samples - 1
    time = last - lax.broadcasted_iota(jnp.int32, (bands, samples), 1)

    def delayed(v, n):
        return jnp.where(time >= n, pltpu.roll(v, samples - n, 1), 0.0)

    resp = jnp.where(time == 0, 1.0, 0.0)
    before = jnp.zeros((bands, 1), F32)
    size = 1
    while size < samples:
        newest = resp[:, samples - size : samples - size + 1]
        following = -a1 * newest - a2 * before
        grown = following * resp - a2 * newest * delayed(resp, 1)
        resp = jnp.where(time < size, resp, delayed(grown, size))
        before = resp[:, samples - 2 * size + 1 : samples - 2 * size + 2]
        size *= 2
    resp = b0 * resp + b1 * delayed(resp, 1) + b2 * delayed(resp, 2)

    def toep_row(t, _):
        row = jnp.where(last - time <= t, pltpu.roll(resp, t + 1, 1), 0.0)
        high, low = split(row)
        at = pl.ds(pl.multiple_of(t * bands, bands), bands)
        toep_ref[at, 0:samples] = high
        toep_ref[at, samples : 2 * samples] = low
        return 0

    lax.fori_loop(0, samples, toep_row, 0, unroll=64)

    slow_id = lax.broadcasted_iota(jnp.int32, (1, slow), 1)
    for i in range(passes):
        for r in range(slots):
            n = i * slots + r
            chosen_ref[n : n + 1, :] = delays_ref[pl.ds(lists_ref[i, r], 1), :]
    pick_ref[...] = jnp.concatenate(
        [jnp.where(slow_id == lists_ref[0, r], 1.0, 0.0) for r in range(slots)], axis=0
    )
    packs_ref[0] = pack[...]
    for copy, sending, receiving in sends:
        pl.when(sending)(copy.wait_send)
        pl.when(receiving)(copy.wait_recv)
    for i in range(1, near + 1):

        @pl.when(me + i < count)
        def _(i=i):
            packs_ref[i] = packs[i - 1]

        @pl.when(me + i >= count)
        def _(i=i):
            packs_ref[i] = jnp.zeros(packs_ref.shape[1:], BF16)

    incoming = jnp.zeros((bands, samples), F32)
    for i in range(count - 1):
        tile = msgs[i, bands : bands + half, :]
        keep = jnp.concatenate([tile[:, 0:1], tile[:, chans // 2 : chans // 2 + 1]], axis=0)
        incoming = keep * incoming + msgs[i, 0:bands, :]
    inc_ref[...] = total_loc * incoming + ends[bands:]


def main_kernel(
    dims, start_ref, packs_ref, inc_ref, toep_ref, hot_ref, chosen_ref, pick_ref, hilbert_ref,
    out_hbm, out2_ref, xt, phases, stacked, lifted, parts3, acc, acc2, power, power2, out_ref, sems,
):
    samples, bands, chans, passes = dims
    slow = hot_ref.shape[2]
    total, aperture = chosen_ref.shape
    slots = total // passes
    blocks = aperture // chans
    offset = lax.rem(start_ref[0], chans)
    points = samples * bands
    pairs = samples // 2
    lags = DMAX // 2

    rows = packs_ref.shape[1]
    lane = lax.broadcasted_iota(jnp.int32, (rows, chans), 1)
    turned = [pltpu.roll(packs_ref[j].astype(F32), chans - offset, 1) for j in range(blocks + 1)]
    window = [
        jnp.where(lane < chans - offset, turned[j], turned[j + 1]) for j in range(blocks)
    ]
    ones = lax.broadcasted_iota(jnp.int32, (chans, chans), 0) <= lax.broadcasted_iota(
        jnp.int32, (chans, chans), 1
    )
    tri = jnp.where(ones, 1.0, 0.0).astype(BF16)
    rise, fall, live, carries = [], [], [], []
    carry = inc_ref[...]
    for j in range(blocks):
        leak = window[j][samples : samples + bands]
        live.append(window[j][samples + bands :])
        alive = (window[j][:samples] * live[j][0:1, :]).astype(BF16)
        stacked[0:samples, j * chans : (j + 1) * chans] = alive
        stacked[samples : 2 * samples, j * chans : (j + 1) * chans] = alive
        summed = jnp.dot(leak.astype(BF16), tri, preferred_element_type=F32)
        middle = 0.5 * summed[:, chans - 1 : chans]
        inflow = inflow_of(leak)
        rise.append(jnp.exp(summed - middle) * inflow)
        fall.append(jnp.exp(middle - summed))
        carries.append(carry * jnp.exp(-middle))
        if j + 1 < blocks:
            high, low = split(jnp.exp(summed - 2.0 * middle) * inflow)
            ends = lax.dot_general(
                jnp.concatenate([high, low], axis=0), alive, NT_DIMS, preferred_element_type=F32
            )
            carry = jnp.exp(-2.0 * middle) * carry + (ends[:bands] + ends[bands:])
    rising = jnp.concatenate(rise, axis=1)
    falling = jnp.concatenate(fall, axis=1)
    living = jnp.concatenate(live, axis=1)

    high, low = split(jnp.concatenate(carries * 2, axis=0))
    twice = jnp.concatenate([high, high], axis=1)
    kinds = 2 * blocks * bands
    lane = lax.broadcasted_iota(jnp.int32, (bands, kinds), 1)
    own = lax.rem(lane, bands) == lax.broadcasted_iota(jnp.int32, (bands, kinds), 0)
    first = lane < blocks * bands

    def every_sample(v):
        return jnp.concatenate([v] * samples, axis=0)

    taps = toep_ref[...]
    filtered = jnp.dot(taps, stacked[...], preferred_element_type=F32).astype(BF16)
    xt[...] = filtered
    lifted[:, 0:aperture] = (filtered.astype(F32) * every_sample(rising)).astype(BF16)
    begin = lax.dot_general(taps, twice, NT_DIMS, preferred_element_type=F32)
    begin += lax.dot_general(taps[:, :samples], low, NT_DIMS, preferred_element_type=F32)
    begin = jnp.where(every_sample(own), begin, 0.0)
    high = begin.astype(BF16).astype(F32)
    lifted[:, aperture:] = jnp.where(every_sample(first), high, begin - high).astype(BF16)

    wide = 2 * chans
    kind = lax.broadcasted_iota(jnp.int32, (kinds, wide), 0)
    place = lax.broadcasted_iota(jnp.int32, (kinds, wide), 1)
    tri_wide = jnp.concatenate(
        [
            jnp.concatenate([tri, jnp.zeros_like(tri)], axis=1),
            jnp.concatenate([jnp.zeros_like(tri), tri], axis=1),
        ],
        axis=0,
    )
    sums_of = [
        jnp.concatenate(
            [
                tri_wide,
                jnp.where(
                    lax.rem(kind // bands, blocks) == 2 * n + place // chans, 1.0, 0.0
                ).astype(BF16),
            ],
            axis=0,
        )
        for n in range(blocks // 2)
    ]
    phases[:, 0:lags] = jnp.zeros((3, lags, bands, aperture), BF16)

    for n in range(blocks // 2):
        cols = slice(n * wide, (n + 1) * wide)
        sums = jnp.dot(
            jnp.concatenate([lifted[:, cols], lifted[:, aperture:]], axis=1),
            sums_of[n],
            preferred_element_type=F32,
        )
        filtered = xt[:, cols].astype(F32)
        d = every_sample(living[:, cols]) * (filtered - every_sample(falling[:, cols]) * sums)
        d = d.astype(BF16)
        xt[:, cols] = d
        d = d.reshape(pairs, 2, bands, wide)
        phases[0, lags:, :, cols] = d[:, 0]
        phases[1, lags:, :, cols] = d[:, 1]
        phases[2, lags:, :, cols] = (d[:, 0].astype(F32) + d[:, 1].astype(F32)).astype(BF16)

    energy = 0.0 * living
    norms = []
    for t in range(samples):
        d = xt[t * bands : (t + 1) * bands, :].astype(F32)
        energy = energy + d * d
        if t >= samples - DMAX:
            norms.insert(0, jnp.sum(energy, axis=0, keepdims=True))

    tiles = slow // LANES
    scale = 1.0 / math.sqrt(aperture)

    def stack(i, _):
        lagged = jnp.concatenate(
            [
                phases[i, lags - q : lags - q + pairs].reshape(pairs * bands, aperture)
                for q in range(lags)
            ],
            axis=1,
        )
        beams = jnp.dot(lagged, hot_ref[i], preferred_element_type=F32) * scale
        parts3[i, bands:, :] = beams
        return 0

    lax.fori_loop(0, 3, stack, 0)
    parts3[1, 0:bands, :] = jnp.zeros((bands, slow), F32)
    for j in range(tiles):
        cols = slice(j * LANES, (j + 1) * LANES)
        even = parts3[0, bands:, cols]
        acc[j, :, 0] = (even + parts3[1, : pairs * bands, cols]).reshape(pairs, bands, LANES)
        odd = parts3[2, bands:, cols] - even - parts3[1, bands:, cols]
        acc[j, :, 1] = odd.reshape(pairs, bands, LANES)
    acc = acc.reshape(tiles, points, LANES)

    def power_of(s):
        turned = jnp.dot(hilbert_ref[...], s.astype(BF16), preferred_element_type=F32)
        return (s * s + turned * turned).T

    pad = jnp.zeros((slots, DMAX * bands), F32)
    length = points + DMAX * bands
    mask = jnp.concatenate([v[0:1, :] for v in live], axis=1)

    def refine(i, guide):
        chosen = chosen_ref[i * slots : (i + 1) * slots, :]
        guide = guide.astype(BF16).astype(F32)
        padded = jnp.concatenate([guide, pad], axis=1)
        shifted = [padded[:, :points]] + [
            pltpu.roll(padded, length - d * bands, 1)[:, :points] for d in range(1, DMAX)
        ]
        shifted = jnp.concatenate(shifted, axis=0).astype(BF16)
        products = jnp.dot(shifted, xt[...], preferred_element_type=F32)
        numerator = jnp.zeros((slots, aperture), F32)
        strength = jnp.zeros((slots, aperture), F32)
        for d in range(DMAX):
            match = chosen == d
            numerator = numerator + jnp.where(match, products[d * slots : (d + 1) * slots, :], 0.0)
            strength = strength + jnp.where(match, norms[d], 0.0)
        guide_norm = jnp.sqrt(jnp.sum(guide * guide, axis=1, keepdims=True) + EPS)
        coherence = numerator / (jnp.sqrt(strength + EPS) * guide_norm)
        weight = mask * (0.25 + jnp.maximum(coherence, 0.0))
        weight = weight.astype(BF16).astype(F32)
        spread = jnp.concatenate(
            [jnp.where(chosen == d, weight, 0.0) for d in range(DMAX)], axis=0
        ).astype(BF16)
        parts = lax.dot_general(spread, xt[...], NT_DIMS, preferred_element_type=F32)
        refined = parts[0:slots, :]
        for d in range(1, DMAX):
            part = jnp.concatenate([parts[d * slots : (d + 1) * slots, :], pad], axis=1)
            refined = refined + pltpu.roll(part, d * bands, 1)[:, :points]
        return refined / jnp.sqrt(1.0 + jnp.sum(weight * weight, axis=1, keepdims=True))

    def envelope(band, _):
        s = jnp.concatenate(
            [acc.at[j][pl.ds(band, samples, stride=bands), :] for j in range(tiles)], axis=1
        )
        power[pl.ds(band, slow, stride=bands), :] = power_of(s)
        return 0

    beams = jnp.concatenate([acc[j].astype(BF16) for j in range(tiles)], axis=1)
    guide = lax.dot_general(pick_ref[...].astype(BF16), beams, NT_DIMS, preferred_element_type=F32)
    results = []
    for i in range(1):
        guide = refine(i, guide)
        results.append(guide)
    lax.fori_loop(0, bands, envelope, 0, unroll=16)
    out_ref[...] = power[...].astype(BF16)
    send = pltpu.make_async_copy(out_ref, out_hbm, sems.at[0])
    send.start()
    for i in range(1, passes):
        guide = refine(i, guide)
        results.append(guide)
    results.append(jnp.zeros((LANES - total, points), F32))
    acc2[...] = jnp.concatenate(results, axis=0).T

    per = LANES // total
    groups = []
    for g in range(bands // per):
        group = acc2[pl.ds(g * per, samples, stride=bands), :]
        for n in range(1, per):
            group += pltpu.roll(acc2[pl.ds(g * per + n, samples, stride=bands), :], n * total, 1)
        groups.append(group)
    both = power_of(jnp.concatenate(groups, axis=1))
    for band in range(bands):
        power2[pl.ds(band, total, stride=bands), :] = both[band * total : (band + 1) * total]
    out2_ref[...] = power2[...].astype(BF16)
    send.wait()


def per_device(traces, filter_coefs, leakage, live_mask, aperture_starts, delays, refine_lists):
    chans, samples = traces.shape
    bands = filter_coefs.shape[0]
    slow, aperture = delays.shape
    near = (aperture + chans - 1) // chans
    count = lax.axis_size("chan")
    passes, slots = refine_lists.shape[1:]
    points = samples * bands
    rows = samples + 2 * bands
    dma = pltpu.SemaphoreType.DMA
    total = passes * slots
    packs, inc, toep, hot, chosen, pick, hilbert = pl.pallas_call(
        functools.partial(exchange_kernel, count, near),
        out_shape=(
            jax.ShapeDtypeStruct((near + 1, rows, chans), BF16),
            jax.ShapeDtypeStruct((bands, samples), F32),
            jax.ShapeDtypeStruct((points, 2 * samples), BF16),
            jax.ShapeDtypeStruct((3, DMAX // 2 * aperture, slow), BF16),
            jax.ShapeDtypeStruct((total, aperture), jnp.int32),
            jax.ShapeDtypeStruct((slots, slow), F32),
            jax.ShapeDtypeStruct((samples, samples), BF16),
        ),
        in_specs=[SM] + [HB] * 7,
        out_specs=(VM,) * 7,
        scratch_shapes=[
            pltpu.SMEM((passes, slots), jnp.int32),
            pltpu.VMEM((chans, samples), BF16),
            pltpu.VMEM((bands, chans), BF16),
            pltpu.VMEM((1, chans), jnp.int32),
            pltpu.VMEM((5, bands), F32),
            pltpu.VMEM((slow, aperture), jnp.int32),
            pltpu.VMEM((rows, chans), BF16),
            pltpu.VMEM((near, rows, chans), BF16),
            pltpu.VMEM((bands + bands // 2, samples), F32),
            pltpu.VMEM((count, bands + bands // 2, samples), F32),
            pltpu.VMEM((aperture, slow), jnp.int32),
            dma((7,)), dma((count,)), dma((count,)), dma((near + 1,)), dma((near + 1,)),
        ],
        compiler_params=pltpu.CompilerParams(
            collective_id=0, has_side_effects=True, vmem_limit_bytes=14 * MIB
        ),
    )(
        aperture_starts,
        *[
            pltpu.with_memory_space_constraint(v, pltpu.HBM)
            for v in (
                refine_lists[0], traces, leakage.T, live_mask[None, :], filter_coefs.T, delays,
                hilbert_table(samples),
            )
        ],
    )
    beam, refined = pl.pallas_call(
        functools.partial(main_kernel, (samples, bands, chans, passes)),
        out_shape=(
            jax.ShapeDtypeStruct((slow * bands, samples), BF16),
            jax.ShapeDtypeStruct((total * bands, samples), BF16),
        ),
        in_specs=[SM] + [VM] * 7,
        out_specs=(HB, VM),
        scratch_shapes=[
            pltpu.VMEM((points, aperture), BF16),
            pltpu.VMEM((3, (samples + DMAX) // 2, bands, aperture), BF16),
            pltpu.VMEM((2 * samples, aperture), BF16),
            pltpu.VMEM((points, aperture + 2 * (aperture // chans) * bands), BF16),
            pltpu.VMEM((3, points // 2 + bands, slow), F32),
            pltpu.VMEM((slow // LANES, samples // 2, 2, bands, LANES), F32),
            pltpu.VMEM((points, LANES), F32),
            pltpu.VMEM((slow * bands, samples), F32),
            pltpu.VMEM((total * bands, samples), F32),
            pltpu.VMEM((slow * bands, samples), BF16),
            dma((1,)),
        ],
        compiler_params=pltpu.CompilerParams(vmem_limit_bytes=32 * MIB),
    )(aperture_starts, packs, inc, toep, hot, chosen, pick, hilbert)
    return (
        beam.reshape(1, slow, bands, samples),
        refined.reshape(1, passes, slots, bands, samples),
    )


def solution(mesh):
    return jax.shard_map(
        per_device,
        mesh=mesh,
        in_specs=(
            P(("cables", "chan"), None),
            P(),
            P(("cables", "chan"), None),
            P(("cables", "chan")),
            P(("cables", "chan")),
            P(),
            P(("cables", "chan"), None, None),
        ),
        out_specs=(
            P(("cables", "chan"), None, None, None),
            P(("cables", "chan"), None, None, None, None),
        ),
        check_vma=False,
    )
```

```python
import functools
import math

import numpy as np

import jax
import jax.numpy as jnp
from jax import lax
from jax.experimental import pallas as pl
from jax.experimental.pallas import tpu as pltpu
from jax.sharding import PartitionSpec as P

DMAX = 16
LANES = 128
EPS = 1e-06
MIB = 1024 * 1024
MESH = pl.DeviceIdType.MESH
VM = pl.BlockSpec(memory_space=pltpu.VMEM)
SM = pl.BlockSpec(memory_space=pltpu.SMEM)
HB = pl.BlockSpec(memory_space=pltpu.HBM)
F32 = jnp.float32
BF16 = jnp.bfloat16
NT_DIMS = (((1,), (1,)), ((), ()))


def hilbert_table(samples):
    index = np.arange(samples)
    offset = (index[:, None] - index[None, :]) % samples
    odd = offset % 2 == 1
    phase = np.pi * offset / samples
    table = np.where(odd, 2.0 / samples * np.cos(phase) / np.where(odd, np.sin(phase), 1.0), 0.0)
    return jnp.asarray(table.astype(np.float32).astype(jnp.bfloat16))


def inflow_of(leak):
    series = leak * (1.0 - leak * (0.5 - leak * (1.0 / 6.0 - leak * (1.0 / 24.0 - leak * (
        1.0 / 120.0 - leak * (1.0 / 720.0 - leak * (1.0 / 5040.0)))))))
    return jnp.where(leak < 0.5, series, 1.0 - jnp.exp(-leak))


def split(x):
    high = x.astype(BF16)
    low = (x - high.astype(F32)).astype(BF16)
    return high, low


def exchange_kernel(
    count, near, start_ref, lists_hbm, x_hbm, leak_hbm, live_hbm, coef_hbm, delays_hbm, hilbert_hbm,
    packs_ref, inc_ref, toep_ref, hot_ref, chosen_ref, pick_ref, hilbert_ref,
    lists_ref, x_ref, leak_ref, live_ref, coef_ref, delays_ref,
    pack, packs, msg, msgs, delt, local, s1, r1, s2, r2,
):
    me = lax.axis_index("chan")
    barrier = pltpu.get_barrier_semaphore()
    for i in range(1, count):
        pl.semaphore_signal(
            barrier, inc=1, device_id={"chan": lax.rem(me + i, count)}, device_id_type=MESH
        )
    loads = [
        pltpu.make_async_copy(src, dst, local.at[n])
        for n, (src, dst) in enumerate(
            [
                (x_hbm, x_ref),
                (leak_hbm, leak_ref),
                (live_hbm, live_ref),
                (coef_hbm, coef_ref),
                (delays_hbm, delays_ref),
                (lists_hbm, lists_ref),
                (hilbert_hbm, hilbert_ref),
            ]
        )
    ]
    for load in loads:
        load.start()
    chans, samples = x_ref.shape
    passes, slots = lists_ref.shape
    bands = leak_ref.shape[0]
    slow, aperture = delays_ref.shape

    for load in loads[:3]:
        load.wait()
    lane = lax.broadcasted_iota(jnp.int32, (bands, chans), 1)
    live = jnp.broadcast_to(live_ref[...], (bands, chans)).astype(F32)
    pack[0:samples, :] = x_ref[...].astype(F32).T.astype(BF16)
    pack[samples : samples + bands, :] = leak_ref[...]
    pack[samples + bands : samples + 2 * bands, :] = live.astype(BF16)

    leak = leak_ref[...].astype(F32)
    inside = lane < start_ref[0] - me * chans
    leak_loc = jnp.where(inside, leak, 0.0)
    later = jnp.where(
        lax.broadcasted_iota(jnp.int32, (chans, chans), 0)
        > lax.broadcasted_iota(jnp.int32, (chans, chans), 1),
        1.0,
        0.0,
    ).astype(BF16)
    suffix = jnp.dot(
        jnp.concatenate([leak, leak_loc], axis=0).astype(BF16), later, preferred_element_type=F32
    )
    gain = inflow_of(leak) * live
    weights = jnp.concatenate([gain, jnp.where(inside, gain, 0.0)], axis=0) * jnp.exp(-suffix)
    high, low = split(weights)
    ends = jnp.dot(jnp.concatenate([high, low], axis=0), x_ref[...], preferred_element_type=F32)
    ends = ends[: 2 * bands] + ends[2 * bands :]
    total = jnp.broadcast_to(jnp.exp(-jnp.sum(leak, axis=1, keepdims=True)), (bands, chans))
    total_loc = jnp.exp(-jnp.sum(leak_loc, axis=1, keepdims=True))
    half = bands // 2
    msg[0:bands, :] = ends[:bands]
    msg[bands : bands + half, :] = jnp.where(lane[:half] < chans // 2, total[:half], total[half:])

    for i in range(count - 1):

        @pl.when(i >= me)
        def _(i=i):
            msgs[i, 0:bands, :] = jnp.zeros((bands, samples), F32)
            msgs[i, bands : bands + half, :] = jnp.ones((half, samples), F32)

    loads[4].wait()
    delt[...] = delays_ref[...].T.astype(F32).astype(BF16)

    def hot_rows(q, _):
        at = pl.ds(pl.multiple_of(q * aperture, aperture), aperture)
        lag = (2 * q).astype(F32)
        here, after = lag.astype(BF16), (lag + 1.0).astype(BF16)
        one, zero = jnp.ones((), BF16), jnp.zeros((), BF16)
        even = jnp.where(delt[...] == here, one, zero)
        odd = jnp.where(delt[...] == after, one, zero)
        hot_ref[0, at, :] = even
        hot_ref[1, at, :] = odd
        hot_ref[2, at, :] = even + odd
        return 0

    lax.fori_loop(0, DMAX // 2, hot_rows, 0)

    pl.semaphore_wait(barrier, count - 1)
    sends = []
    for i in [*range(1, near + 1)][::-1]:
        sends.append(
            (
                pltpu.make_async_remote_copy(
                    src_ref=pack,
                    dst_ref=packs.at[i - 1],
                    send_sem=s2.at[i],
                    recv_sem=r2.at[i],
                    device_id={"chan": lax.rem(me + count - i, count)},
                    device_id_type=MESH,
                ),
                me - i >= 0,
                me + i < count,
            )
        )
    for i in [*range(1, count)][::-1]:
        sends.append(
            (
                pltpu.make_async_remote_copy(
                    src_ref=msg,
                    dst_ref=msgs.at[me],
                    send_sem=s1.at[i],
                    recv_sem=r1.at[i],
                    device_id={"chan": lax.rem(me + i, count)},
                    device_id_type=MESH,
                ),
                me + i < count,
                me - i >= 0,
            )
        )
    for copy, sending, _ in sends:
        pl.when(sending)(copy.start)

    for load in (loads[3], loads[5], loads[6]):
        load.wait()
    eye = lax.broadcasted_iota(jnp.int32, (bands, bands), 0) == lax.broadcasted_iota(
        jnp.int32, (bands, bands), 1
    )
    b0, b1, b2, a1, a2 = [
        jnp.sum(jnp.where(eye, coef_ref[i : i + 1, :], 0.0), axis=1, keepdims=True) for i in range(5)
    ]
    last = samples - 1
    time = last - lax.broadcasted_iota(jnp.int32, (bands, samples), 1)

    def delayed(v, n):
        return jnp.where(time >= n, pltpu.roll(v, samples - n, 1), 0.0)

    resp = jnp.where(time == 0, 1.0, 0.0)
    before = jnp.zeros((bands, 1), F32)
    size = 1
    while size < samples:
        newest = resp[:, samples - size : samples - size + 1]
        following = -a1 * newest - a2 * before
        grown = following * resp - a2 * newest * delayed(resp, 1)
        resp = jnp.where(time < size, resp, delayed(grown, size))
        before = resp[:, samples - 2 * size + 1 : samples - 2 * size + 2]
        size *= 2
    resp = b0 * resp + b1 * delayed(resp, 1) + b2 * delayed(resp, 2)

    high, low = split(resp)

    def toep_row(t, _):
        at = pl.ds(pl.multiple_of(t * bands, bands), bands)
        reach = last - time <= t
        toep_ref[at, 0:samples] = jnp.where(reach, pltpu.roll(high, t + 1, 1), jnp.zeros_like(high))
        toep_ref[at, samples : 2 * samples] = jnp.where(
            reach, pltpu.roll(low, t + 1, 1), jnp.zeros_like(low)
        )
        return 0

    lax.fori_loop(0, samples, toep_row, 0, unroll=64)

    slow_id = lax.broadcasted_iota(jnp.int32, (1, slow), 1)
    for i in range(passes):
        for r in range(slots):
            n = i * slots + r
            chosen_ref[n : n + 1, :] = delays_ref[pl.ds(lists_ref[i, r], 1), :]
    pick_ref[...] = jnp.concatenate(
        [jnp.where(slow_id == lists_ref[0, r], 1.0, 0.0) for r in range(slots)], axis=0
    )
    packs_ref[0] = pack[...]
    for copy, _, receiving in sends:
        pl.when(receiving)(copy.wait_recv)
    for i in range(1, near + 1):

        @pl.when(me + i < count)
        def _(i=i):
            packs_ref[i] = packs[i - 1]

        @pl.when(me + i >= count)
        def _(i=i):
            packs_ref[i] = jnp.zeros(packs_ref.shape[1:], BF16)

    incoming = jnp.zeros((bands, samples), F32)
    for i in range(count - 1):
        tile = msgs[i, bands : bands + half, :]
        keep = jnp.concatenate([tile[:, 0:1], tile[:, chans // 2 : chans // 2 + 1]], axis=0)
        incoming = keep * incoming + msgs[i, 0:bands, :]
    inc_ref[...] = total_loc * incoming + ends[bands:]
    for copy, sending, _ in sends:
        pl.when(sending)(copy.wait_send)


def main_kernel(
    dims, start_ref, packs_ref, inc_ref, toep_ref, hot_ref, chosen_ref, pick_ref, hilbert_ref,
    out_hbm, out2_ref, xt, phases, stacked, lifted, parts3, acc, acc2, power, power2, out_ref, sems,
):
    samples, bands, chans, passes = dims
    slow = hot_ref.shape[2]
    total, aperture = chosen_ref.shape
    slots = total // passes
    blocks = aperture // chans
    offset = lax.rem(start_ref[0], chans)
    points = samples * bands
    pairs = samples // 2
    lags = DMAX // 2

    rows = packs_ref.shape[1]
    lane = lax.broadcasted_iota(jnp.int32, (rows, chans), 1)
    turned = [pltpu.roll(packs_ref[j].astype(F32), chans - offset, 1) for j in range(blocks + 1)]
    window = [
        jnp.where(lane < chans - offset, turned[j], turned[j + 1]) for j in range(blocks)
    ]
    ones = lax.broadcasted_iota(jnp.int32, (chans, chans), 0) <= lax.broadcasted_iota(
        jnp.int32, (chans, chans), 1
    )
    tri = jnp.where(ones, 1.0, 0.0).astype(BF16)
    rise, fall, live, carries = [], [], [], []
    carry = inc_ref[...]
    for j in range(blocks):
        leak = window[j][samples : samples + bands]
        live.append(window[j][samples + bands :])
        alive = (window[j][:samples] * live[j][0:1, :]).astype(BF16)
        stacked[0:samples, j * chans : (j + 1) * chans] = alive
        stacked[samples : 2 * samples, j * chans : (j + 1) * chans] = alive
        summed = jnp.dot(leak.astype(BF16), tri, preferred_element_type=F32)
        middle = 0.5 * summed[:, chans - 1 : chans]
        inflow = inflow_of(leak)
        rise.append(jnp.exp(summed - middle) * inflow)
        fall.append(jnp.exp(middle - summed))
        carries.append(carry * jnp.exp(-middle))
        if j + 1 < blocks:
            high, low = split(jnp.exp(summed - 2.0 * middle) * inflow)
            ends = lax.dot_general(
                jnp.concatenate([high, low], axis=0), alive, NT_DIMS, preferred_element_type=F32
            )
            carry = jnp.exp(-2.0 * middle) * carry + (ends[:bands] + ends[bands:])
    rising = jnp.concatenate(rise, axis=1)
    falling = jnp.concatenate(fall, axis=1)
    living = jnp.concatenate(live, axis=1)

    high, low = split(jnp.concatenate(carries * 2, axis=0))
    twice = jnp.concatenate([high, high], axis=1)
    kinds = 2 * blocks * bands
    lane = lax.broadcasted_iota(jnp.int32, (bands, kinds), 1)
    own = lax.rem(lane, bands) == lax.broadcasted_iota(jnp.int32, (bands, kinds), 0)
    first = lane < blocks * bands

    def every_sample(v):
        return jnp.concatenate([v] * samples, axis=0)

    taps = toep_ref[...]
    filtered = jnp.dot(taps, stacked[...], preferred_element_type=F32).astype(BF16)
    xt[...] = filtered
    lifted[:, 0:aperture] = (filtered.astype(F32) * every_sample(rising)).astype(BF16)
    begin = lax.dot_general(taps, twice, NT_DIMS, preferred_element_type=F32)
    begin += lax.dot_general(taps[:, :samples], low, NT_DIMS, preferred_element_type=F32)
    begin = jnp.where(every_sample(own), begin, 0.0)
    high = begin.astype(BF16).astype(F32)
    lifted[:, aperture:] = jnp.where(every_sample(first), high, begin - high).astype(BF16)

    wide = 2 * chans
    kind = lax.broadcasted_iota(jnp.int32, (kinds, wide), 0)
    place = lax.broadcasted_iota(jnp.int32, (kinds, wide), 1)
    tri_wide = jnp.concatenate(
        [
            jnp.concatenate([tri, jnp.zeros_like(tri)], axis=1),
            jnp.concatenate([jnp.zeros_like(tri), tri], axis=1),
        ],
        axis=0,
    )
    sums_of = [
        jnp.concatenate(
            [
                tri_wide,
                jnp.where(
                    lax.rem(kind // bands, blocks) == 2 * n + place // chans, 1.0, 0.0
                ).astype(BF16),
            ],
            axis=0,
        )
        for n in range(blocks // 2)
    ]
    phases[:, 0:lags] = jnp.zeros((3, lags, bands, aperture), BF16)

    for n in range(blocks // 2):
        cols = slice(n * wide, (n + 1) * wide)
        sums = jnp.dot(
            jnp.concatenate([lifted[:, cols], lifted[:, aperture:]], axis=1),
            sums_of[n],
            preferred_element_type=F32,
        )
        filtered = xt[:, cols].astype(F32)
        d = every_sample(living[:, cols]) * (filtered - every_sample(falling[:, cols]) * sums)
        d = d.astype(BF16)
        xt[:, cols] = d
        d = d.reshape(pairs, 2, bands, wide)
        phases[0, lags:, :, cols] = d[:, 0]
        phases[1, lags:, :, cols] = d[:, 1]
        phases[2, lags:, :, cols] = (d[:, 0].astype(F32) + d[:, 1].astype(F32)).astype(BF16)

    energy = 0.0 * living
    norms = []
    for t in range(samples):
        d = xt[t * bands : (t + 1) * bands, :].astype(F32)
        energy = energy + d * d
        if t >= samples - DMAX:
            norms.insert(0, jnp.sum(energy, axis=0, keepdims=True))

    tiles = slow // LANES
    scale = 1.0 / math.sqrt(aperture)

    def stack(i, _):
        lagged = jnp.concatenate(
            [
                phases[i, lags - q : lags - q + pairs].reshape(pairs * bands, aperture)
                for q in range(lags)
            ],
            axis=1,
        )
        beams = jnp.dot(lagged, hot_ref[i], preferred_element_type=F32) * scale
        parts3[i, bands:, :] = beams
        return 0

    lax.fori_loop(0, 3, stack, 0)
    parts3[1, 0:bands, :] = jnp.zeros((bands, slow), F32)
    for j in range(tiles):
        cols = slice(j * LANES, (j + 1) * LANES)
        even = parts3[0, bands:, cols]
        acc[j, :, 0] = (even + parts3[1, : pairs * bands, cols]).reshape(pairs, bands, LANES)
        odd = parts3[2, bands:, cols] - even - parts3[1, bands:, cols]
        acc[j, :, 1] = odd.reshape(pairs, bands, LANES)
    acc = acc.reshape(tiles, points, LANES)

    def power_of(s):
        turned = jnp.dot(hilbert_ref[...], s.astype(BF16), preferred_element_type=F32)
        return (s * s + turned * turned).T

    pad = jnp.zeros((slots, DMAX * bands), F32)
    length = points + DMAX * bands
    mask = jnp.concatenate([v[0:1, :] for v in live], axis=1)

    def refine(i, guide):
        chosen = chosen_ref[i * slots : (i + 1) * slots, :]
        guide = guide.astype(BF16).astype(F32)
        padded = jnp.concatenate([guide, pad], axis=1)
        shifted = [padded[:, :points]] + [
            pltpu.roll(padded, length - d * bands, 1)[:, :points] for d in range(1, DMAX)
        ]
        shifted = jnp.concatenate(shifted, axis=0).astype(BF16)
        products = jnp.dot(shifted, xt[...], preferred_element_type=F32)
        numerator = jnp.zeros((slots, aperture), F32)
        strength = jnp.zeros((slots, aperture), F32)
        for d in range(DMAX):
            match = chosen == d
            numerator = numerator + jnp.where(match, products[d * slots : (d + 1) * slots, :], 0.0)
            strength = strength + jnp.where(match, norms[d], 0.0)
        guide_norm = jnp.sqrt(jnp.sum(guide * guide, axis=1, keepdims=True) + EPS)
        coherence = numerator / (jnp.sqrt(strength + EPS) * guide_norm)
        weight = mask * (0.25 + jnp.maximum(coherence, 0.0))
        weight = weight.astype(BF16).astype(F32)
        spread = jnp.concatenate(
            [jnp.where(chosen == d, weight, 0.0) for d in range(DMAX)], axis=0
        ).astype(BF16)
        parts = lax.dot_general(spread, xt[...], NT_DIMS, preferred_element_type=F32)
        refined = parts[0:slots, :]
        for d in range(1, DMAX):
            part = jnp.concatenate([parts[d * slots : (d + 1) * slots, :], pad], axis=1)
            refined = refined + pltpu.roll(part, d * bands, 1)[:, :points]
        return refined / jnp.sqrt(1.0 + jnp.sum(weight * weight, axis=1, keepdims=True))

    def envelope(band, _):
        s = jnp.concatenate(
            [acc.at[j][pl.ds(band, samples, stride=bands), :] for j in range(tiles)], axis=1
        )
        power[pl.ds(band, slow, stride=bands), :] = power_of(s)
        return 0

    beams = jnp.concatenate([acc[j].astype(BF16) for j in range(tiles)], axis=1)
    guide = lax.dot_general(pick_ref[...].astype(BF16), beams, NT_DIMS, preferred_element_type=F32)
    results = []
    for i in range(1):
        guide = refine(i, guide)
        results.append(guide)
    lax.fori_loop(0, bands, envelope, 0, unroll=16)
    out_ref[...] = power[...].astype(BF16)
    send = pltpu.make_async_copy(out_ref, out_hbm, sems.at[0])
    send.start()
    for i in range(1, passes):
        guide = refine(i, guide)
        results.append(guide)
    results.append(jnp.zeros((LANES - total, points), F32))
    acc2[...] = jnp.concatenate(results, axis=0).T

    per = LANES // total
    groups = []
    for g in range(bands // per):
        group = acc2[pl.ds(g * per, samples, stride=bands), :]
        for n in range(1, per):
            group += pltpu.roll(acc2[pl.ds(g * per + n, samples, stride=bands), :], n * total, 1)
        groups.append(group)
    both = power_of(jnp.concatenate(groups, axis=1))
    for band in range(bands):
        power2[pl.ds(band, total, stride=bands), :] = both[band * total : (band + 1) * total]
    out2_ref[...] = power2[...].astype(BF16)
    send.wait()


def per_device(traces, filter_coefs, leakage, live_mask, aperture_starts, delays, refine_lists):
    chans, samples = traces.shape
    bands = filter_coefs.shape[0]
    slow, aperture = delays.shape
    near = (aperture + chans - 1) // chans
    count = lax.axis_size("chan")
    passes, slots = refine_lists.shape[1:]
    points = samples * bands
    rows = samples + 2 * bands
    dma = pltpu.SemaphoreType.DMA
    total = passes * slots
    packs, inc, toep, hot, chosen, pick, hilbert = pl.pallas_call(
        functools.partial(exchange_kernel, count, near),
        out_shape=(
            jax.ShapeDtypeStruct((near + 1, rows, chans), BF16),
            jax.ShapeDtypeStruct((bands, samples), F32),
            jax.ShapeDtypeStruct((points, 2 * samples), BF16),
            jax.ShapeDtypeStruct((3, DMAX // 2 * aperture, slow), BF16),
            jax.ShapeDtypeStruct((total, aperture), jnp.int32),
            jax.ShapeDtypeStruct((slots, slow), F32),
            jax.ShapeDtypeStruct((samples, samples), BF16),
        ),
        in_specs=[SM] + [HB] * 7,
        out_specs=(VM,) * 7,
        scratch_shapes=[
            pltpu.SMEM((passes, slots), jnp.int32),
            pltpu.VMEM((chans, samples), BF16),
            pltpu.VMEM((bands, chans), BF16),
            pltpu.VMEM((1, chans), jnp.int32),
            pltpu.VMEM((5, bands), F32),
            pltpu.VMEM((slow, aperture), jnp.int32),
            pltpu.VMEM((rows, chans), BF16),
            pltpu.VMEM((near, rows, chans), BF16),
            pltpu.VMEM((bands + bands // 2, samples), F32),
            pltpu.VMEM((count, bands + bands // 2, samples), F32),
            pltpu.VMEM((aperture, slow), BF16),
            dma((7,)), dma((count,)), dma((count,)), dma((near + 1,)), dma((near + 1,)),
        ],
        compiler_params=pltpu.CompilerParams(
            collective_id=0, has_side_effects=True, vmem_limit_bytes=14 * MIB
        ),
    )(
        aperture_starts,
        *[
            pltpu.with_memory_space_constraint(v, pltpu.HBM)
            for v in (
                refine_lists[0], traces, leakage.T, live_mask[None, :], filter_coefs.T, delays,
                hilbert_table(samples),
            )
        ],
    )
    beam, refined = pl.pallas_call(
        functools.partial(main_kernel, (samples, bands, chans, passes)),
        out_shape=(
            jax.ShapeDtypeStruct((slow * bands, samples), BF16),
            jax.ShapeDtypeStruct((total * bands, samples), BF16),
        ),
        in_specs=[SM] + [VM] * 7,
        out_specs=(HB, VM),
        scratch_shapes=[
            pltpu.VMEM((points, aperture), BF16),
            pltpu.VMEM((3, (samples + DMAX) // 2, bands, aperture), BF16),
            pltpu.VMEM((2 * samples, aperture), BF16),
            pltpu.VMEM((points, aperture + 2 * (aperture // chans) * bands), BF16),
            pltpu.VMEM((3, points // 2 + bands, slow), F32),
            pltpu.VMEM((slow // LANES, samples // 2, 2, bands, LANES), F32),
            pltpu.VMEM((points, LANES), F32),
            pltpu.VMEM((slow * bands, samples), F32),
            pltpu.VMEM((total * bands, samples), F32),
            pltpu.VMEM((slow * bands, samples), BF16),
            dma((1,)),
        ],
        compiler_params=pltpu.CompilerParams(vmem_limit_bytes=32 * MIB),
    )(aperture_starts, packs, inc, toep, hot, chosen, pick, hilbert)
    return (
        beam.reshape(1, slow, bands, samples),
        refined.reshape(1, passes, slots, bands, samples),
    )


def solution(mesh):
    return jax.shard_map(
        per_device,
        mesh=mesh,
        in_specs=(
            P(("cables", "chan"), None),
            P(),
            P(("cables", "chan"), None),
            P(("cables", "chan")),
            P(("cables", "chan")),
            P(),
            P(("cables", "chan"), None, None),
        ),
        out_specs=(
            P(("cables", "chan"), None, None, None),
            P(("cables", "chan"), None, None, None, None),
        ),
        check_vma=False,
    )
```

```python
import functools
import math

import numpy as np

import jax
import jax.numpy as jnp
from jax import lax
from jax.experimental import pallas as pl
from jax.experimental.pallas import tpu as pltpu
from jax.sharding import PartitionSpec as P

DMAX = 16
LANES = 128
EPS = 1e-06
MIB = 1024 * 1024
MESH = pl.DeviceIdType.MESH
VM = pl.BlockSpec(memory_space=pltpu.VMEM)
SM = pl.BlockSpec(memory_space=pltpu.SMEM)
HB = pl.BlockSpec(memory_space=pltpu.HBM)
F32 = jnp.float32
BF16 = jnp.bfloat16
NT_DIMS = (((1,), (1,)), ((), ()))


def hilbert_table(samples):
    index = np.arange(samples)
    offset = (index[:, None] - index[None, :]) % samples
    odd = offset % 2 == 1
    phase = np.pi * offset / samples
    table = np.where(odd, 2.0 / samples * np.cos(phase) / np.where(odd, np.sin(phase), 1.0), 0.0)
    return jnp.asarray(table.astype(np.float32).astype(jnp.bfloat16))


def inflow_of(leak):
    series = leak * (1.0 - leak * (0.5 - leak * (1.0 / 6.0 - leak * (1.0 / 24.0 - leak * (
        1.0 / 120.0 - leak * (1.0 / 720.0 - leak * (1.0 / 5040.0)))))))
    return jnp.where(leak < 0.5, series, 1.0 - jnp.exp(-leak))


def split(x):
    high = x.astype(BF16)
    low = (x - high.astype(F32)).astype(BF16)
    return high, low


def exchange_kernel(
    count, near, start_ref, lists_hbm, x_hbm, leak_hbm, live_hbm, coef_hbm, delays_hbm, hilbert_hbm,
    packs_ref, inc_ref, toep_ref, hot_ref, chosen_ref, pick_ref, hilbert_ref,
    lists_ref, x_ref, leak_ref, live_ref, coef_ref, delays_ref,
    pack, packs, msg, msgs, delt, local, s1, r1, s2, r2,
):
    me = lax.axis_index("chan")
    barrier = pltpu.get_barrier_semaphore()
    for i in range(1, count):
        pl.semaphore_signal(
            barrier, inc=1, device_id={"chan": lax.rem(me + i, count)}, device_id_type=MESH
        )
    loads = [
        pltpu.make_async_copy(src, dst, local.at[n])
        for n, (src, dst) in enumerate(
            [
                (x_hbm, x_ref),
                (leak_hbm, leak_ref),
                (live_hbm, live_ref),
                (coef_hbm, coef_ref),
                (delays_hbm, delays_ref),
                (lists_hbm, lists_ref),
                (hilbert_hbm, hilbert_ref),
            ]
        )
    ]
    for load in loads:
        load.start()
    chans, samples = x_ref.shape
    passes, slots = lists_ref.shape
    bands = leak_ref.shape[0]
    slow, aperture = delays_ref.shape

    for load in loads[:3]:
        load.wait()
    lane = lax.broadcasted_iota(jnp.int32, (bands, chans), 1)
    live = jnp.broadcast_to(live_ref[...], (bands, chans)).astype(F32)
    pack[0:samples, :] = x_ref[...].astype(F32).T.astype(BF16)
    pack[samples : samples + bands, :] = leak_ref[...]
    pack[samples + bands : samples + 2 * bands, :] = live.astype(BF16)

    leak = leak_ref[...].astype(F32)
    inside = lane < start_ref[0] - me * chans
    leak_loc = jnp.where(inside, leak, 0.0)
    later = jnp.where(
        lax.broadcasted_iota(jnp.int32, (chans, chans), 0)
        > lax.broadcasted_iota(jnp.int32, (chans, chans), 1),
        1.0,
        0.0,
    ).astype(BF16)
    suffix = jnp.dot(
        jnp.concatenate([leak, leak_loc], axis=0).astype(BF16), later, preferred_element_type=F32
    )
    gain = inflow_of(leak) * live
    weights = jnp.concatenate([gain, jnp.where(inside, gain, 0.0)], axis=0) * jnp.exp(-suffix)
    high, low = split(weights)
    ends = jnp.dot(jnp.concatenate([high, low], axis=0), x_ref[...], preferred_element_type=F32)
    ends = ends[: 2 * bands] + ends[2 * bands :]
    total = jnp.broadcast_to(jnp.exp(-jnp.sum(leak, axis=1, keepdims=True)), (bands, chans))
    total_loc = jnp.exp(-jnp.sum(leak_loc, axis=1, keepdims=True))
    half = bands // 2
    msg[0:bands, :] = ends[:bands]
    msg[bands : bands + half, :] = jnp.where(lane[:half] < chans // 2, total[:half], total[half:])

    for i in range(count - 1):

        @pl.when(i >= me)
        def _(i=i):
            msgs[i, 0:bands, :] = jnp.zeros((bands, samples), F32)
            msgs[i, bands : bands + half, :] = jnp.ones((half, samples), F32)

    loads[4].wait()
    delt[...] = delays_ref[...].T.astype(F32).astype(BF16)

    def hot_rows(q, _):
        at = pl.ds(pl.multiple_of(q * aperture, aperture), aperture)
        lag = (2 * q).astype(F32)
        here, after = lag.astype(BF16), (lag + 1.0).astype(BF16)
        one, zero = jnp.ones((), BF16), jnp.zeros((), BF16)
        even = jnp.where(delt[...] == here, one, zero)
        odd = jnp.where(delt[...] == after, one, zero)
        hot_ref[0, at, :] = even
        hot_ref[1, at, :] = odd
        hot_ref[2, at, :] = even + odd
        return 0

    lax.fori_loop(0, DMAX // 2, hot_rows, 0)

    pl.semaphore_wait(barrier, count - 1)
    sends = []
    for i in [*range(1, near + 1)][::-1]:
        sends.append(
            (
                pltpu.make_async_remote_copy(
                    src_ref=pack,
                    dst_ref=packs.at[i - 1],
                    send_sem=s2.at[i],
                    recv_sem=r2.at[i],
                    device_id={"chan": lax.rem(me + count - i, count)},
                    device_id_type=MESH,
                ),
                me - i >= 0,
                me + i < count,
            )
        )
    for i in [*range(1, count)][::-1]:
        sends.append(
            (
                pltpu.make_async_remote_copy(
                    src_ref=msg,
                    dst_ref=msgs.at[me],
                    send_sem=s1.at[i],
                    recv_sem=r1.at[i],
                    device_id={"chan": lax.rem(me + i, count)},
                    device_id_type=MESH,
                ),
                me + i < count,
                me - i >= 0,
            )
        )
    for copy, sending, _ in sends:
        pl.when(sending)(copy.start)

    for load in (loads[3], loads[5], loads[6]):
        load.wait()
    eye = lax.broadcasted_iota(jnp.int32, (bands, bands), 0) == lax.broadcasted_iota(
        jnp.int32, (bands, bands), 1
    )
    b0, b1, b2, a1, a2 = [
        jnp.sum(jnp.where(eye, coef_ref[i : i + 1, :], 0.0), axis=1, keepdims=True) for i in range(5)
    ]
    last = samples - 1
    time = last - lax.broadcasted_iota(jnp.int32, (bands, samples), 1)

    def delayed(v, n):
        return jnp.where(time >= n, pltpu.roll(v, samples - n, 1), 0.0)

    resp = jnp.where(time == 0, 1.0, 0.0)
    before = jnp.zeros((bands, 1), F32)
    size = 1
    while size < samples:
        newest = resp[:, samples - size : samples - size + 1]
        following = -a1 * newest - a2 * before
        grown = following * resp - a2 * newest * delayed(resp, 1)
        resp = jnp.where(time < size, resp, delayed(grown, size))
        before = resp[:, samples - 2 * size + 1 : samples - 2 * size + 2]
        size *= 2
    resp = b0 * resp + b1 * delayed(resp, 1) + b2 * delayed(resp, 2)

    high, low = split(resp)

    def toep_row(t, _):
        at = pl.ds(pl.multiple_of(t * bands, bands), bands)
        reach = last - time <= t
        toep_ref[at, 0:samples] = jnp.where(reach, pltpu.roll(high, t + 1, 1), jnp.zeros_like(high))
        toep_ref[at, samples : 2 * samples] = jnp.where(
            reach, pltpu.roll(low, t + 1, 1), jnp.zeros_like(low)
        )
        return 0

    lax.fori_loop(0, samples, toep_row, 0, unroll=64)

    slow_id = lax.broadcasted_iota(jnp.int32, (1, slow), 1)
    for i in range(passes):
        for r in range(slots):
            n = i * slots + r
            chosen_ref[n : n + 1, :] = delays_ref[pl.ds(lists_ref[i, r], 1), :]
    pick_ref[...] = jnp.concatenate(
        [jnp.where(slow_id == lists_ref[0, r], 1.0, 0.0) for r in range(slots)], axis=0
    )
    packs_ref[0] = pack[...]
    for copy, _, receiving in sends:
        pl.when(receiving)(copy.wait_recv)
    for i in range(1, near + 1):

        @pl.when(me + i < count)
        def _(i=i):
            packs_ref[i] = packs[i - 1]

        @pl.when(me + i >= count)
        def _(i=i):
            packs_ref[i] = jnp.zeros(packs_ref.shape[1:], BF16)

    incoming = jnp.zeros((bands, samples), F32)
    for i in range(count - 1):
        tile = msgs[i, bands : bands + half, :]
        keep = jnp.concatenate([tile[:, 0:1], tile[:, chans // 2 : chans // 2 + 1]], axis=0)
        incoming = keep * incoming + msgs[i, 0:bands, :]
    inc_ref[...] = total_loc * incoming + ends[bands:]
    for copy, sending, _ in sends:
        pl.when(sending)(copy.wait_send)


def main_kernel(
    dims, start_ref, packs_ref, inc_ref, toep_ref, hot_ref, chosen_ref, pick_ref, hilbert_ref,
    out_hbm, out2_ref, xt, phases, stacked, lifted, parts3, acc, acc2, power, power2, out_ref, sems,
):
    samples, bands, chans, passes = dims
    slow = hot_ref.shape[2]
    total, aperture = chosen_ref.shape
    slots = total // passes
    blocks = aperture // chans
    offset = lax.rem(start_ref[0], chans)
    points = samples * bands
    pairs = samples // 2
    lags = DMAX // 2

    rows = packs_ref.shape[1]
    lane = lax.broadcasted_iota(jnp.int32, (rows, chans), 1)
    turned = [pltpu.roll(packs_ref[j].astype(F32), chans - offset, 1) for j in range(blocks + 1)]
    window = [
        jnp.where(lane < chans - offset, turned[j], turned[j + 1]) for j in range(blocks)
    ]
    ones = lax.broadcasted_iota(jnp.int32, (chans, chans), 0) <= lax.broadcasted_iota(
        jnp.int32, (chans, chans), 1
    )
    tri = jnp.where(ones, 1.0, 0.0).astype(BF16)
    rise, fall, live, carries = [], [], [], []
    carry = inc_ref[...]
    for j in range(blocks):
        leak = window[j][samples : samples + bands]
        live.append(window[j][samples + bands :])
        alive = (window[j][:samples] * live[j][0:1, :]).astype(BF16)
        stacked[0:samples, j * chans : (j + 1) * chans] = alive
        stacked[samples : 2 * samples, j * chans : (j + 1) * chans] = alive
        summed = jnp.dot(leak.astype(BF16), tri, preferred_element_type=F32)
        middle = 0.5 * summed[:, chans - 1 : chans]
        inflow = inflow_of(leak)
        rise.append(jnp.exp(summed - middle) * inflow)
        fall.append(jnp.exp(middle - summed))
        carries.append(carry * jnp.exp(-middle))
        if j + 1 < blocks:
            high, low = split(jnp.exp(summed - 2.0 * middle) * inflow)
            ends = lax.dot_general(
                jnp.concatenate([high, low], axis=0), alive, NT_DIMS, preferred_element_type=F32
            )
            carry = jnp.exp(-2.0 * middle) * carry + (ends[:bands] + ends[bands:])
    rising = jnp.concatenate(rise, axis=1)
    falling = jnp.concatenate(fall, axis=1)
    living = jnp.concatenate(live, axis=1)

    high, low = split(jnp.concatenate(carries * 2, axis=0))
    twice = jnp.concatenate([high, high], axis=1)
    kinds = 2 * blocks * bands
    lane = lax.broadcasted_iota(jnp.int32, (bands, kinds), 1)
    own = lax.rem(lane, bands) == lax.broadcasted_iota(jnp.int32, (bands, kinds), 0)
    first = lane < blocks * bands

    def every_sample(v):
        return jnp.concatenate([v] * samples, axis=0)

    taps = toep_ref[...]
    filtered = jnp.dot(taps, stacked[...], preferred_element_type=F32).astype(BF16)
    xt[...] = filtered
    lifted[:, 0:aperture] = (filtered.astype(F32) * every_sample(rising)).astype(BF16)
    begin = lax.dot_general(taps, twice, NT_DIMS, preferred_element_type=F32)
    begin += lax.dot_general(taps[:, :samples], low, NT_DIMS, preferred_element_type=F32)
    begin = jnp.where(every_sample(own), begin, 0.0)
    high = begin.astype(BF16).astype(F32)
    lifted[:, aperture:] = jnp.where(every_sample(first), high, begin - high).astype(BF16)

    wide = 2 * chans
    kind = lax.broadcasted_iota(jnp.int32, (kinds, wide), 0)
    place = lax.broadcasted_iota(jnp.int32, (kinds, wide), 1)
    tri_wide = jnp.concatenate(
        [
            jnp.concatenate([tri, jnp.zeros_like(tri)], axis=1),
            jnp.concatenate([jnp.zeros_like(tri), tri], axis=1),
        ],
        axis=0,
    )
    sums_of = [
        jnp.concatenate(
            [
                tri_wide,
                jnp.where(
                    lax.rem(kind // bands, blocks) == 2 * n + place // chans, 1.0, 0.0
                ).astype(BF16),
            ],
            axis=0,
        )
        for n in range(blocks // 2)
    ]
    phases[:, 0:lags] = jnp.zeros((3, lags, bands, aperture), BF16)

    for n in range(blocks // 2):
        cols = slice(n * wide, (n + 1) * wide)
        sums = jnp.dot(
            jnp.concatenate([lifted[:, cols], lifted[:, aperture:]], axis=1),
            sums_of[n],
            preferred_element_type=F32,
        )
        filtered = xt[:, cols].astype(F32)
        d = every_sample(living[:, cols]) * (filtered - every_sample(falling[:, cols]) * sums)
        d = d.astype(BF16)
        xt[:, cols] = d
        d = d.reshape(pairs, 2, bands, wide)
        phases[0, lags:, :, cols] = d[:, 0]
        phases[1, lags:, :, cols] = d[:, 1]
        phases[2, lags:, :, cols] = (d[:, 0].astype(F32) + d[:, 1].astype(F32)).astype(BF16)

    energy = 0.0 * living
    norms = []
    for t in range(samples):
        d = xt[t * bands : (t + 1) * bands, :].astype(F32)
        energy = energy + d * d
        if t >= samples - DMAX:
            norms.insert(0, jnp.sum(energy, axis=0, keepdims=True))

    strengths = jnp.zeros((total, aperture), F32)
    for d in range(DMAX):
        strengths = strengths + jnp.where(chosen_ref[...] == d, norms[d], 0.0)
    strengths = jnp.sqrt(strengths + EPS)

    tiles = slow // LANES
    scale = 1.0 / math.sqrt(aperture)

    def stack(i, _):
        lagged = jnp.concatenate(
            [
                phases[i, lags - q : lags - q + pairs].reshape(pairs * bands, aperture)
                for q in range(lags)
            ],
            axis=1,
        )
        beams = jnp.dot(lagged, hot_ref[i], preferred_element_type=F32)
        parts3[i, bands:, :] = beams
        return 0

    lax.fori_loop(0, 3, stack, 0)
    parts3[1, 0:bands, :] = jnp.zeros((bands, slow), F32)
    for j in range(tiles):
        cols = slice(j * LANES, (j + 1) * LANES)
        even = parts3[0, bands:, cols]
        acc[j, :, 0] = (scale * (even + parts3[1, : pairs * bands, cols])).reshape(pairs, bands, LANES)
        odd = scale * (parts3[2, bands:, cols] - even - parts3[1, bands:, cols])
        acc[j, :, 1] = odd.reshape(pairs, bands, LANES)
    acc = acc.reshape(tiles, points, LANES)

    def power_of(s):
        turned = jnp.dot(hilbert_ref[...], s.astype(BF16), preferred_element_type=F32)
        return (s * s + turned * turned).T

    pad = jnp.zeros((slots, DMAX * bands), F32)
    length = points + DMAX * bands
    mask = jnp.concatenate([v[0:1, :] for v in live], axis=1)

    def refine(i, guide):
        chosen = chosen_ref[i * slots : (i + 1) * slots, :]
        guide = guide.astype(BF16).astype(F32)
        padded = jnp.concatenate([guide, pad], axis=1)
        shifted = [padded[:, :points]] + [
            pltpu.roll(padded, length - d * bands, 1)[:, :points] for d in range(1, DMAX)
        ]
        shifted = jnp.concatenate(shifted, axis=0).astype(BF16)
        products = jnp.dot(shifted, xt[...], preferred_element_type=F32)
        numerator = jnp.zeros((slots, aperture), F32)
        strength = strengths[i * slots : (i + 1) * slots, :]
        for d in range(DMAX):
            match = chosen == d
            numerator = numerator + jnp.where(match, products[d * slots : (d + 1) * slots, :], 0.0)
        guide_norm = jnp.sqrt(jnp.sum(guide * guide, axis=1, keepdims=True) + EPS)
        coherence = numerator / (strength * guide_norm)
        weight = mask * (0.25 + jnp.maximum(coherence, 0.0))
        weight = weight.astype(BF16).astype(F32)
        spread = jnp.concatenate(
            [jnp.where(chosen == d, weight, 0.0) for d in range(DMAX)], axis=0
        ).astype(BF16)
        parts = lax.dot_general(spread, xt[...], NT_DIMS, preferred_element_type=F32)
        refined = parts[0:slots, :]
        for d in range(1, DMAX):
            part = jnp.concatenate([parts[d * slots : (d + 1) * slots, :], pad], axis=1)
            refined = refined + pltpu.roll(part, d * bands, 1)[:, :points]
        return refined / jnp.sqrt(1.0 + jnp.sum(weight * weight, axis=1, keepdims=True))

    def envelope(band, _):
        s = jnp.concatenate(
            [acc.at[j][pl.ds(band, samples, stride=bands), :] for j in range(tiles)], axis=1
        )
        power[pl.ds(band, slow, stride=bands), :] = power_of(s)
        return 0

    beams = jnp.concatenate([acc[j].astype(BF16) for j in range(tiles)], axis=1)
    guide = lax.dot_general(pick_ref[...].astype(BF16), beams, NT_DIMS, preferred_element_type=F32)
    results = []
    for i in range(1):
        guide = refine(i, guide)
        results.append(guide)
    lax.fori_loop(0, bands, envelope, 0, unroll=16)
    out_ref[...] = power[...].astype(BF16)
    send = pltpu.make_async_copy(out_ref, out_hbm, sems.at[0])
    send.start()
    for i in range(1, passes):
        guide = refine(i, guide)
        results.append(guide)
    results.append(jnp.zeros((LANES - total, points), F32))
    acc2[...] = jnp.concatenate(results, axis=0).T

    per = LANES // total
    groups = []
    for g in range(bands // per):
        group = acc2[pl.ds(g * per, samples, stride=bands), :]
        for n in range(1, per):
            group += pltpu.roll(acc2[pl.ds(g * per + n, samples, stride=bands), :], n * total, 1)
        groups.append(group)
    both = power_of(jnp.concatenate(groups, axis=1))
    for band in range(bands):
        power2[pl.ds(band, total, stride=bands), :] = both[band * total : (band + 1) * total]
    out2_ref[...] = power2[...].astype(BF16)
    send.wait()


def per_device(traces, filter_coefs, leakage, live_mask, aperture_starts, delays, refine_lists):
    chans, samples = traces.shape
    bands = filter_coefs.shape[0]
    slow, aperture = delays.shape
    near = (aperture + chans - 1) // chans
    count = lax.axis_size("chan")
    passes, slots = refine_lists.shape[1:]
    points = samples * bands
    rows = samples + 2 * bands
    dma = pltpu.SemaphoreType.DMA
    total = passes * slots
    packs, inc, toep, hot, chosen, pick, hilbert = pl.pallas_call(
        functools.partial(exchange_kernel, count, near),
        out_shape=(
            jax.ShapeDtypeStruct((near + 1, rows, chans), BF16),
            jax.ShapeDtypeStruct((bands, samples), F32),
            jax.ShapeDtypeStruct((points, 2 * samples), BF16),
            jax.ShapeDtypeStruct((3, DMAX // 2 * aperture, slow), BF16),
            jax.ShapeDtypeStruct((total, aperture), jnp.int32),
            jax.ShapeDtypeStruct((slots, slow), F32),
            jax.ShapeDtypeStruct((samples, samples), BF16),
        ),
        in_specs=[SM] + [HB] * 7,
        out_specs=(VM,) * 7,
        scratch_shapes=[
            pltpu.SMEM((passes, slots), jnp.int32),
            pltpu.VMEM((chans, samples), BF16),
            pltpu.VMEM((bands, chans), BF16),
            pltpu.VMEM((1, chans), jnp.int32),
            pltpu.VMEM((5, bands), F32),
            pltpu.VMEM((slow, aperture), jnp.int32),
            pltpu.VMEM((rows, chans), BF16),
            pltpu.VMEM((near, rows, chans), BF16),
            pltpu.VMEM((bands + bands // 2, samples), F32),
            pltpu.VMEM((count, bands + bands // 2, samples), F32),
            pltpu.VMEM((aperture, slow), BF16),
            dma((7,)), dma((count,)), dma((count,)), dma((near + 1,)), dma((near + 1,)),
        ],
        compiler_params=pltpu.CompilerParams(
            collective_id=0, has_side_effects=True, vmem_limit_bytes=14 * MIB
        ),
    )(
        aperture_starts,
        *[
            pltpu.with_memory_space_constraint(v, pltpu.HBM)
            for v in (
                refine_lists[0], traces, leakage.T, live_mask[None, :], filter_coefs.T, delays,
                hilbert_table(samples),
            )
        ],
    )
    beam, refined = pl.pallas_call(
        functools.partial(main_kernel, (samples, bands, chans, passes)),
        out_shape=(
            jax.ShapeDtypeStruct((slow * bands, samples), BF16),
            jax.ShapeDtypeStruct((total * bands, samples), BF16),
        ),
        in_specs=[SM] + [VM] * 7,
        out_specs=(HB, VM),
        scratch_shapes=[
            pltpu.VMEM((points, aperture), BF16),
            pltpu.VMEM((3, (samples + DMAX) // 2, bands, aperture), BF16),
            pltpu.VMEM((2 * samples, aperture), BF16),
            pltpu.VMEM((points, aperture + 2 * (aperture // chans) * bands), BF16),
            pltpu.VMEM((3, points // 2 + bands, slow), F32),
            pltpu.VMEM((slow // LANES, samples // 2, 2, bands, LANES), F32),
            pltpu.VMEM((points, LANES), F32),
            pltpu.VMEM((slow * bands, samples), F32),
            pltpu.VMEM((total * bands, samples), F32),
            pltpu.VMEM((slow * bands, samples), BF16),
            dma((1,)),
        ],
        compiler_params=pltpu.CompilerParams(vmem_limit_bytes=32 * MIB),
    )(aperture_starts, packs, inc, toep, hot, chosen, pick, hilbert)
    return (
        beam.reshape(1, slow, bands, samples),
        refined.reshape(1, passes, slots, bands, samples),
    )


def solution(mesh):
    return jax.shard_map(
        per_device,
        mesh=mesh,
        in_specs=(
            P(("cables", "chan"), None),
            P(),
            P(("cables", "chan"), None),
            P(("cables", "chan")),
            P(("cables", "chan")),
            P(),
            P(("cables", "chan"), None, None),
        ),
        out_specs=(
            P(("cables", "chan"), None, None, None),
            P(("cables", "chan"), None, None, None, None),
        ),
        check_vma=False,
    )
```
